32 devices in a mesh: apa: 2 (over y), gz: 4 (over x, core), drift: 4 (over z).
Axes of the slice: x: 2, y: 2, z: 4, core: 2. Of those that a mesh axis runs over, the one named last changes fastest.
Arguments:
- charge: bfloat16 [16384, 384], P(('apa', 'gz', 'drift')), parts along dimension 0, may hold values from 0.049804688 to 2
- intersection: bfloat16 [128, 3, 2, 32, 128], P(('apa', 'gz', 'drift')), parts along dimension 0, may hold values from 0 to 0.03125
- ovl_block: int32 [128, 3, 2], P(('apa', 'gz', 'drift')), parts along dimension 0, may hold values from 0 to 15, as said below
- ovl_count: int32 [128, 3], P(('apa', 'gz', 'drift')), parts along dimension 0, may hold values from 1 to 2
- diff_class: int32 [768], P('apa'), parts along dimension 0, may hold values from 0 to 5
- response: bfloat16 [3, 21, 200], replicated, may hold values from -0.029907227 to 0.029907227
- cotangent: bfloat16 [6, 512, 3072], P('apa', 'gz', 'drift'), parts along dimension 0, may hold values from -120 to 120
Outputs:
- signal: bfloat16 [6, 512, 3072], P('apa', 'gz', 'drift'), parts along dimension 0
- charge_grad: bfloat16 [16384, 384], P(('apa', 'gz', 'drift')), parts along dimension 0
The draws below stay inside these ranges and needn't reach their ends.
There are 2 independent parts, one for each index of `apa`. The reference program is written for one: setup_inputs(seed, part) draws one part's arguments, and reference() takes and returns one part's arrays. A program takes and returns all parts, laid end to end along the dimension named above; an argument that names none is the same for every part. Nothing has to cross between parts.
Inputs may be any that keep to these rules, and one draw needn't show every extreme that they name: `ovl_block`: planes are U, V, W in this order. Cell block b lies in z-block b // 16; its W entries name wire blocks of that z-block, z-block g owning wire blocks g * 4 to (g + 1) * 4 - 1 of every plane. Entry 0 of each list is live. Among the live U and V entries of one group of 4 consecutive cell blocks (starting at a multiple of 4), at most 8 name wire blocks of one z-block, and every such group reaches 8 for some z-block. `ovl_count`: entry k of a list is live where k < count; the others are ignored.
All inputs are finite; a program needn't handle non-finite values.
Results may differ from the reference program's by a relative error of at most 0.0058.
Values may be sent and summed in bfloat16 or wider, within the bound.
A program may use at most 128 MiB of HBM per device.

```python
import math
import jax
import jax.numpy as jnp
from jax import lax

WIRES = 512
TICKS = 3072
RESP_W = 21
RESP_T = 200
WB = 32
TPB = 8
HB = 2
K = 2
VB = 128
NDIFF = 6
NVB = 4
WBLK = 16
X = 384
VBLK = 64
CELLS = 8192
N_GZ = 4
N_DRIFT = 4


def draw_ovl_block(key, part):
    devices = N_GZ * N_DRIFT
    per_owner = WIRES // WB // N_GZ
    cap_limit = 8 * NVB // N_GZ
    other_count = N_GZ - 1
    key_hot, key_order, key_shift, key_cross, key_local = jax.random.split(jax.random.fold_in(key, 17), 5)
    hot_rows = jax.random.randint(key_hot, (N_DRIFT,), 0, N_GZ)
    device_ids = jnp.arange(devices, dtype=jnp.int32)
    z_block = device_ids // N_DRIFT
    hot_owner = hot_rows[device_ids % N_DRIFT][:, None]
    slot_order = jax.vmap(lambda single: jax.random.permutation(single, 2 * NVB))(jax.random.split(key_order, devices))
    slot_rank = jnp.argsort(slot_order, axis=1).astype(jnp.int32)
    owner_shift = jax.random.randint(key_shift, (devices, 1), 0, other_count)
    first_owner = jnp.where(slot_rank < cap_limit, hot_owner, (hot_owner + 1 + (slot_rank - cap_limit + owner_shift) % other_count) % N_GZ)
    later_index = 2 * NVB - cap_limit + jnp.arange(2 * NVB, dtype=jnp.int32)[None, :]
    second_owner = (hot_owner + 1 + (later_index + owner_shift) % other_count) % N_GZ
    owners = jnp.stack([first_owner, second_owner], axis=-1)
    cross_blocks = owners * per_owner + jax.random.randint(key_cross, owners.shape, 0, per_owner)
    cross_blocks = cross_blocks.reshape(devices, NVB, 2, 2)
    local_blocks = z_block[:, None, None, None] * per_owner + jax.random.randint(key_local, (devices, NVB, 1, 2), 0, per_owner)
    return jnp.concatenate([cross_blocks, local_blocks], axis=2).reshape(devices * NVB, 3, 2).astype(jnp.int32)


def place_ends(result, rng, smallest, largest):
    extent = result.shape
    place = [jax.random.randint(jax.random.fold_in(rng, axis), (), 0, extent[axis]) for axis in range(len(extent))]
    result = result.at[tuple(place)].set(smallest)
    longest = extent.index(max(extent))
    place[longest] = (place[longest] + 1) % extent[longest]
    return result.at[tuple(place)].set(largest)


def level_of(key, extent, cuts, least, largest):
    loudness = 1.0
    for position, blocks in cuts:
        draws = jax.random.uniform(jax.random.fold_in(jax.random.fold_in(key, 6), position), (blocks,), jnp.float32, least / len(cuts), largest / len(cuts))
        loudness = loudness * jnp.repeat(jnp.exp(draws), extent[position] // blocks).reshape((-1,) + (1,) * (len(extent) - 1 - position))
    return loudness


def gaussian(own_key, extent, scale, reach, cuts=(), kind=jnp.bfloat16):
    array = jax.random.normal(own_key, extent, jnp.float32) * scale
    if len(cuts) > 0:
        array = level_of(own_key, extent, cuts, -0.22, 0.18) * array
    return jnp.clip(array, min=-reach, max=reach).astype(kind)


def setup_inputs(seed: int = 0, part: int = 0) -> dict:
    arg_keys = jax.random.split(jax.random.key(seed), 8)
    own_keys = jax.random.split(jax.random.fold_in(arg_keys[7], part), 8)
    return {
        "charge": jnp.clip(jnp.exp(math.log(2.0) - 3.6927934 * jax.random.uniform(own_keys[0], (CELLS, X), jnp.float32) ** level_of(own_keys[0], (CELLS, X), ((0, 16),), -0.2, 0.2)), 0.049804688, 2.0).astype(jnp.bfloat16),
        "intersection": jnp.clip(0.03125 * jax.random.uniform(own_keys[1], (VBLK, 3, K, WB, VB), jnp.float32) ** level_of(own_keys[1], (VBLK, 3, K, WB, VB), ((0, 16),), -0.2, 0.2), 0.0, 0.03125).astype(jnp.bfloat16),
        "ovl_block": draw_ovl_block(jax.random.fold_in(jax.random.fold_in(arg_keys[7], part), 71), part),
        "ovl_count": place_ends(jax.random.randint(own_keys[3], (VBLK, 3), 1, K + 1), jax.random.fold_in(own_keys[3], 1), 1, K).astype(jnp.int32),
        "diff_class": place_ends(jax.random.randint(own_keys[4], (X,), 0, NDIFF), jax.random.fold_in(own_keys[4], 1), 0, NDIFF - 1).astype(jnp.int32),
        "response": gaussian(arg_keys[5], (3, RESP_W, RESP_T), 0.005, 0.029907227),
        "cotangent": gaussian(own_keys[6], (3, WIRES, TICKS), 20.0, 120.0, ((1, 4), (2, 4))),
    }


def smear_weights(offset, classes):
    spread_width = TPB * (0.2 + 0.15 * classes)
    reach_ticks = HB * TPB
    samples = jnp.arange(-reach_ticks, reach_ticks).astype(jnp.float32) + 0.5
    normalizer = jnp.sum(jnp.exp(-(samples * samples) / (2.0 * spread_width[..., None] * spread_width[..., None])), axis=-1)
    inside = jnp.abs(offset) < reach_ticks
    bump = jnp.exp(-(offset * offset) / (2.0 * spread_width * spread_width))
    return jnp.where(inside, bump, jnp.zeros_like(bump)) / normalizer


def planes_conv(field, kernel, padding):
    return lax.conv_general_dilated(field[None], kernel[:, None], (1, 1), padding, dimension_numbers=("NCHW", "OIHW", "NCHW"), feature_group_count=3, precision=lax.Precision.HIGHEST)[0]


def reference(charge, intersection, ovl_block, ovl_count, diff_class, response, cotangent):
    highest = lax.Precision.HIGHEST
    entry_live = jnp.arange(K, dtype=jnp.int32)[None, None, :] < ovl_count[:, :, None]
    weights = intersection.astype(jnp.float32)
    charge_blocks = charge.reshape(VBLK, VB, X).astype(jnp.float32)
    pieces = jnp.einsum("bpkwc,bcx->bpkwx", weights, charge_blocks, precision=highest).astype(jnp.bfloat16)
    pieces = jnp.where(entry_live[:, :, :, None, None], pieces, jnp.zeros((), jnp.bfloat16))
    plane_of = jnp.broadcast_to(jnp.arange(3, dtype=jnp.int32)[None, :, None], ovl_block.shape)
    target = (plane_of * WBLK + ovl_block).reshape(-1).astype(jnp.int32)
    currents = jax.ops.segment_sum(pieces.reshape(VBLK * 3 * K, WB, X).astype(jnp.float32), target, num_segments=3 * WBLK)
    currents = currents.reshape(3, WIRES, X)
    bin_index = jnp.arange(X).astype(jnp.float32)
    tick_index = jnp.arange(TICKS).astype(jnp.float32)
    offset = tick_index[None, :] - TPB * bin_index[:, None] - (TPB - 1) / 2.0
    smear_table = smear_weights(offset, diff_class.astype(jnp.float32)[:, None])
    drifted = jnp.einsum("pwx,xt->pwt", currents, smear_table, precision=highest).astype(jnp.bfloat16)
    half_width = (RESP_W - 1) // 2
    response_wide = response.astype(jnp.float32)
    signal = planes_conv(drifted.astype(jnp.float32), response_wide[:, :, ::-1], [(half_width, half_width), (RESP_T - 1, 0)]).astype(jnp.bfloat16)
    tick_grads = planes_conv(cotangent.astype(jnp.float32), response_wide[:, ::-1, :], [(half_width, half_width), (0, RESP_T - 1)]).astype(jnp.bfloat16)
    bin_grads = jnp.einsum("pwt,xt->pwx", tick_grads.astype(jnp.float32), smear_table, precision=highest).astype(jnp.bfloat16)
    blocks = bin_grads.reshape(3 * WBLK, WB, X)
    chosen = jnp.take(blocks, target, axis=0).reshape(VBLK, 3, K, WB, X)
    chosen = jnp.where(entry_live[:, :, :, None, None], chosen, jnp.zeros((), jnp.bfloat16))
    charge_grad = jnp.einsum("bpkwc,bpkwx->bcx", weights, chosen.astype(jnp.float32), precision=highest)
    return signal, charge_grad.reshape(CELLS, X).astype(jnp.bfloat16)
```

```python
import functools
import math

import jax
import jax.numpy as jnp
from jax import lax
from jax.experimental import pallas as pl
from jax.experimental.pallas import tpu as pltpu
from jax.sharding import PartitionSpec as P

TPB = 8
HB = 2
LIMIT = 44
LANES = 128
ROWS = 16
WIN = 64
NDIFF = 6
MESH = pl.DeviceIdType.MESH
F32 = jnp.float32
BF16 = jnp.bfloat16

VMEM = pl.BlockSpec(memory_space=pltpu.VMEM)
SMEM = pl.BlockSpec(memory_space=pltpu.SMEM)
HBM = pl.BlockSpec(memory_space=pltpu.HBM)

REACH = HB * TPB
LOW = -(REACH - (TPB - 1) // 2 - 1)


def round_up(value, step):
    return -(-value // step) * step


def iota(shape, dim):
    return lax.broadcasted_iota(jnp.int32, shape, dim)


def dot(left, right, contract=((1,), (0,))):
    return lax.dot_general(left, right, (contract, ((), ())), preferred_element_type=F32)


def class_scale(k):
    width = TPB * (0.2 + 0.15 * k)
    return 1.0 / (2.0 * width * width)


def class_norm(k):
    return sum(math.exp(-((j + 0.5) ** 2) * class_scale(k)) for j in range(-REACH, REACH))


def kernel(
    cfg,
    blk_hbm,
    cnt_hbm,
    charge_hbm,
    inter_hbm,
    class_hbm,
    resp_hbm,
    cot_hbm,
    sig_ref,
    grad_ref,
    blk_ref,
    cnt_ref,
    charge_ref,
    inter_ref,
    class_ref,
    resp_ref,
    cot_ref,
    load_s,
    round_s,
    spread_ref,
    own_ref,
    csend_ref,
    crecv_ref,
    xsend_ref,
    xrecv_ref,
    place_ref,
    zsend_ref,
    zrecv_ref,
    zgate_ref,
    zsum_ref,
    hrecv_ref,
    chalo_ref,
    every_ref,
    spread_t_ref,
    taps_ref,
    table_ref,
    green_ref,
    wide_ref,
    field_ref,
    pair_ref,
    total_ref,
    core_s,
    core_r,
    x_s,
    x_r,
    z_s,
    z_r,
    zg_r,
    h_s,
    h_r,
    c_s,
    c_r,
    ga_r,
    gr_s,
    gx_s,
    gx_r,
    gc_s,
):
    owners, slabs, front, pairs, block = cfg
    blocks, planes, entries, wires, cells = inter_ref.shape
    bins = charge_ref.shape[1]
    here, ticks_here = cot_ref.shape[1:]
    spread, length = resp_ref.shape[1:]
    per_owner = here // wires
    bins_here = bins // slabs
    half = (spread - 1) // 2
    chips = owners // 2
    rows = 2 * here
    chunks = ticks_here // block
    slots = 2 * pairs

    z = lax.axis_index("drift")
    g = lax.axis_index("gz")
    core = g % 2
    chip = g // 2
    partner = g + 1 - 2 * core

    def remote(src, dst, send, recv, gz, drift):
        return pltpu.make_async_remote_copy(
            src_ref=src,
            dst_ref=dst,
            send_sem=send,
            recv_sem=recv,
            device_id={"gz": gz, "drift": drift},
            device_id_type=MESH,
        )

    loads = [
        pltpu.make_async_copy(src, dst, load_s.at[n])
        for n, (src, dst) in enumerate(
            (
                (blk_hbm, blk_ref),
                (cnt_hbm, cnt_ref),
                (inter_hbm, inter_ref),
                (charge_hbm, charge_ref),
                (class_hbm, class_ref),
                (resp_hbm, resp_ref),
                (cot_hbm, cot_ref),
            )
        )
    ]
    for load in loads:
        load.start()

    barrier = pltpu.get_barrier_semaphore()

    def greet(sem, gz, drift):
        pl.semaphore_signal(
            sem, inc=1, device_id={"gz": gz, "drift": drift}, device_id_type=MESH
        )

    has_prev = g > 0
    has_next = g < owners - 1
    sides = has_prev.astype(jnp.int32) + has_next.astype(jnp.int32)
    has_left = z > 0
    has_right = z < slabs - 1
    rounds = chips == 2 and slabs <= 4

    def near(sem):
        for j in range(1, chips):
            greet(sem, ((chip + j) % chips) * 2 + core, z)
        if rounds:

            @pl.when(has_left)
            def _():
                greet(sem, g, z - 1)

            @pl.when(has_right)
            def _():
                greet(sem, g, z + 1)

        else:
            for j in range(1, slabs):
                greet(sem, g, (z + j) % slabs)
        here_only = [z] if rounds else list(range(slabs))

        @pl.when(has_prev)
        def _():
            for d in here_only:
                greet(sem, g - 1, d)

        @pl.when(has_next)
        def _():
            for d in here_only:
                greet(sem, g + 1, d)

    ends = has_left.astype(jnp.int32) + has_right.astype(jnp.int32)
    if rounds:
        near_count = (chips - 1) + ends + sides
    else:
        near_count = (chips - 1) + (slabs - 1) + slabs * sides
    near(barrier)

    def second_round():
        if rounds:
            near(round_s.at[0])

    def third_round():
        if rounds:
            pl.semaphore_wait(round_s.at[0], near_count)
            for step in (1, 2):

                @pl.when(z >= step)
                def _():
                    greet(round_s.at[1], g, z - step)

                @pl.when(z + step < slabs)
                def _():
                    greet(round_s.at[1], g, z + step)

    def all_here():
        if rounds:
            count = 0
            for step in (1, 2):
                count += (z >= step).astype(jnp.int32) + (z + step < slabs).astype(jnp.int32)
            pl.semaphore_wait(round_s.at[1], count)

    for load in loads[:3]:
        load.wait()
    def spread_block(block_index, p, at):
        for b in range(blocks):
            total = jnp.zeros((wires, cells), BF16)
            for k in range(entries):
                named = (blk_ref[p, k, b] == block_index) & (k < cnt_ref[b, p])
                total = total + jnp.where(named, inter_ref[b, p, k], jnp.zeros((wires, cells), BF16))
            spread_ref[pl.ds(at, wires), b * cells : (b + 1) * cells] = total

    def spread_owner(owner, _):
        for p in range(2):
            for q in range(per_owner):
                spread_block(
                    owner * per_owner + q,
                    p,
                    pl.multiple_of(owner * rows + (p * per_owner + q) * wires, wires),
                )
        return 0

    lax.fori_loop(0, owners, spread_owner, 0)
    for q in range(per_owner):
        spread_block(g * per_owner + q, 2, owners * rows + q * wires)

    loads[3].wait()
    charge = charge_ref[...]
    for k in range(chips):
        there = pl.multiple_of((2 * k + 1 - core) * rows, rows)
        csend_ref[k] = dot(spread_ref[pl.ds(there, rows), :], charge).astype(BF16)

    depth = round_up(length, ROWS)
    loads[4].wait()
    loads[5].wait()
    taps_ref[...] = jnp.zeros_like(taps_ref)
    for p in range(planes):
        taps_ref[p, 0:spread, 0:length] = resp_ref[p].astype(F32)
    taps = taps_ref[...].reshape(planes * taps_ref.shape[1], taps_ref.shape[2]).astype(BF16)
    row_class = class_ref[...].reshape(1, bins)
    tables = NDIFF + 2
    delta = iota((depth, 2 * LANES), 1) - iota((depth, 2 * LANES), 0)
    offset = (delta + LOW).astype(F32) - (TPB - 1) / 2
    inside = jnp.abs(offset) < REACH
    squared = offset * offset
    for k in range(tables):
        if k < NDIFF:
            scale, norm = class_scale(k), class_norm(k)
            keep = inside
        else:
            first = row_class[:, k - NDIFF : k - NDIFF + 1]
            scale = jnp.zeros((1, 1), F32)
            norm = jnp.zeros((1, 1), F32)
            for c in range(NDIFF):
                scale += jnp.where(first == c, class_scale(c), 0.0)
                norm += jnp.where(first == c, class_norm(c), 0.0)
            keep = inside & (delta + LOW + TPB * (k - NDIFF) >= 0)
        smear = jnp.where(keep, jnp.exp(-squared * scale), 0.0) / norm
        upper = smear.astype(BF16)
        lower = (smear - upper.astype(F32)).astype(BF16)
        spot = pl.ds(k, taps.shape[0], stride=tables)
        filtered = dot(taps, upper) + dot(taps, lower)
        table_ref[0, spot, :] = filtered[:, :LANES]
        table_ref[1, spot, :] = filtered[:, LANES:]

    bin_of = iota((LANES, bins), 0) + bins_here * z - front
    chosen = jnp.where(iota((LANES, bins), 1) == bin_of, 1.0, 0.0).astype(BF16)
    bin_row = iota((tables, bins), 1)
    table_row = iota((tables, bins), 0)
    wanted = jnp.where(bin_row < 2, NDIFF + bin_row, row_class)
    uses = jnp.where(table_row == wanted, 1.0, 0.0).astype(BF16)
    pick = dot(chosen, uses, ((1,), (1,))).astype(BF16)

    start = (LOW - TPB * front) % LANES
    blocks_of = LANES // TPB
    turn = iota((LANES, LANES), 0) % blocks_of * TPB + start
    right = iota((LANES, LANES), 1) >= turn
    group = slots // 2

    def split(value):
        upper = value.astype(BF16)
        return upper, (value - upper.astype(F32)).astype(BF16)

    def green_rows(p, part, step):
        j0 = step * group
        for u in range(group):
            j = j0 + u
            at = pl.multiple_of((p * taps_ref.shape[1] + j) * tables, tables)
            one, two = (
                pltpu.roll(
                    dot(pick, split(table_ref[n, pl.ds(at, tables), :])[part]),
                    start,
                    1,
                    stride=TPB,
                    stride_axis=0,
                )
                for n in range(2)
            )
            outs = (
                jnp.where(right, one, 0.0).astype(BF16),
                jnp.where(right, two, one).astype(BF16),
                jnp.where(right, 0.0, two).astype(BF16),
                jnp.zeros((LANES, LANES), BF16),
            )
            for q in range(LANES // blocks_of):
                here_rows = slice(q * blocks_of, (q + 1) * blocks_of)
                base = q - (TPB * front - LOW + start) // LANES
                for n in range(4):
                    lanes = (base + n) % 4 * LANES
                    green_ref[part, p, j, here_rows, lanes : lanes + LANES] = outs[n][here_rows]

    def green(p, part):
        def half_of(step, _):
            green_rows(p, part, step)
            return 0

        lax.fori_loop(0, 2, half_of, 0)

    def operator(p, c, half_of=0):
        first = block * c // TPB
        lanes = block * c % (4 * LANES)
        part = green_ref[half_of, p, :, first : first + WIN, lanes : lanes + block]
        return part.reshape(slots * WIN, block)

    pl.semaphore_wait(barrier, near_count)
    second_round()

    def core_copy(k):
        return remote(
            csend_ref.at[k], crecv_ref.at[k], core_s.at[k], core_r.at[k], partner, z
        )

    for j in range(1, chips + 1):
        core_copy((chip + j) % chips).start()

    def cot_down():
        return remote(
            cot_hbm.at[:, 0:ROWS], chalo_ref.at[1], c_s.at[1], c_r.at[1], g - 1, z
        )

    def cot_up():
        return remote(
            cot_hbm.at[:, here - ROWS : here], chalo_ref.at[0], c_s.at[0], c_r.at[0], g + 1, z
        )

    @pl.when(has_prev)
    def _():
        cot_down().start()

    @pl.when(has_next)
    def _():
        cot_up().start()

    @pl.when(g == 0)
    def _():
        chalo_ref[0] = jnp.zeros(chalo_ref.shape[1:], BF16)
        hrecv_ref[0] = jnp.zeros(hrecv_ref.shape[1:], BF16)

    @pl.when(g == owners - 1)
    def _():
        chalo_ref[1] = jnp.zeros(chalo_ref.shape[1:], BF16)
        hrecv_ref[1] = jnp.zeros(hrecv_ref.shape[1:], BF16)

    lane = iota((bins, slabs * LANES), 1)
    place_ref[...] = jnp.where(
        iota((bins, slabs * LANES), 0)
        == (lane // LANES) * bins_here - front + lane % LANES,
        1.0,
        0.0,
    ).astype(BF16)

    mid = slabs // 2
    low_half = z < mid
    base = jnp.where(low_half, 0, mid)
    base_there = mid - base
    gate = jnp.where(low_half, mid - 1, mid)
    gate_there = slabs - 1 - gate
    is_gate = z == gate

    def in_half(j):
        return base + (z - base + j) % mid

    def frame(p, sums):
        framed = dot(sums.astype(BF16), place_ref[...]).astype(BF16)
        for d in range(slabs):
            zsend_ref[d, p] = framed[:, d * LANES : (d + 1) * LANES]

    def half_copy(j, p):
        return remote(
            zsend_ref.at[in_half(j), p],
            zrecv_ref.at[j - 1, p],
            z_s.at[0],
            z_r.at[j - 1, p],
            g,
            in_half(j),
        )

    giver = jnp.where(low_half, z, z - mid - 1)

    def gate_copy(i, p):
        return remote(
            zsend_ref.at[base_there + i, p],
            zgate_ref.at[jnp.clip(giver, 0, mid - 2), i, p],
            z_s.at[1],
            zg_r.at[jnp.clip(giver, 0, mid - 2), p],
            g,
            gate,
        )

    def arrived(ref, sem):
        remote(ref, ref, z_s.at[0], sem, g, z).wait_recv()

    def sent(ref, sem):
        remote(ref, ref, sem, z_r.at[0, 0], g, z).wait_send()

    def sum_copy(i, p):
        return remote(
            zsum_ref.at[i, p],
            zrecv_ref.at[mid - 1, p],
            z_s.at[2],
            z_r.at[mid - 1, p],
            g,
            base_there + i,
        )

    def edge_copy(side, j, p):
        rows_of = slice(here - ROWS, here) if side == 0 else slice(0, ROWS)
        return remote(
            zsend_ref.at[in_half(j), p, rows_of],
            hrecv_ref.at[side, j, p],
            h_s.at[side],
            h_r.at[side, p],
            g + 1 if side == 0 else g - 1,
            in_half(j),
        )

    def edge_sum(side, i, p):
        rows_of = slice(here - ROWS, here) if side == 0 else slice(0, ROWS)
        return remote(
            zsum_ref.at[i, p, rows_of],
            hrecv_ref.at[side, mid, p],
            h_s.at[2 + side],
            h_r.at[side, p],
            g + 1 if side == 0 else g - 1,
            base_there + i,
        )

    def edges(side):
        return has_next if side == 0 else has_prev

    def send_windows(p):
        @pl.when(jnp.logical_not(is_gate))
        def _():
            for i in range(mid):
                gate_copy(i, p).start()

        for j in range(1, mid):
            half_copy(j, p).start()
        for side in range(2):

            @pl.when(edges(side))
            def _():
                for j in range(mid):
                    edge_copy(side, j, p).start()

    def gate_sums(p):
        @pl.when(is_gate)
        def _():
            for n in range(mid - 1):
                arrived(zgate_ref.at[n, :, p], zg_r.at[n, p])
            for i in range(mid):
                total = zsend_ref[base_there + i, p].astype(F32)
                for n in range(mid - 1):
                    total += zgate_ref[n, i, p].astype(F32)
                zsum_ref[i, p] = total.astype(BF16)
                sum_copy(i, p).start()
            for side in range(2):

                @pl.when(edges(side))
                def _():
                    for i in range(mid):
                        edge_sum(side, i, p).start()

    def own_parts():
        frame(2, dot(spread_ref[owners * rows : owners * rows + here, :], charge))
        for k in range(chips):
            there = pl.multiple_of((2 * k + core) * rows, rows)
            own_ref[k] = dot(spread_ref[pl.ds(there, rows), :], charge)

    turned = here % LANES == 0

    def turn_shares():
        if turned:
            for n in range(spread_ref.shape[0] // LANES):
                part = slice(n * LANES, (n + 1) * LANES)
                spread_t_ref[:, part] = spread_ref[part, :].T

    def x_copy(j, p):
        return remote(
            xsend_ref.at[j - 1, p],
            xrecv_ref.at[j - 1, p],
            x_s.at[j - 1, p],
            x_r.at[j - 1, p],
            ((chip + j) % chips) * 2 + core,
            z,
        )

    def core_sums():
        for j in range(1, chips):
            k = (chip + j) % chips
            core_copy(k).wait_recv()
            for p in range(2):
                part = pl.ds(p * here, here)
                xsend_ref[j - 1, p] = (
                    own_ref[k, part, :] + crecv_ref[k, part, :].astype(F32)
                ).astype(BF16)
                x_copy(j, p).start()

    def place_of(owner, p):
        at = owner * rows + p * here if p < 2 else owners * rows
        return pl.ds(pl.multiple_of(at, here), here)

    def block_at(d, owner, p):
        return every_ref.at[d, place_of(owner, p)]

    def ag_copy(j, p):
        part = block_at(z, g, p)
        to = in_half(j) if j else gate_there
        return remote(part, part, z_s.at[3], ga_r.at[z, p], g, to)

    def ag_pass(i, j, p):
        d = base_there + i
        part = block_at(d, g, p)
        return remote(part, part, gr_s.at[j - 1], ga_r.at[d, p], g, in_half(j))

    def ag_wait(d, p):
        part = block_at(d, g, p)
        arrived(part, ga_r.at[d, p])

    def gx_copy(j, d, p, owner):
        part = block_at(d, owner, p)
        return remote(
            part,
            part,
            gx_s.at[j - 1],
            gx_r.at[j - 1, d, p],
            ((chip + j) % chips) * 2 + core,
            z,
        )

    def gc_copy(d, p, owner):
        part = block_at(d, owner, p)
        return remote(part, part, gc_s.at[0], gc_s.at[1], partner, z)

    def spread_bins(d, p):
        if p < 2:
            for j in range(1, chips):
                gx_copy(j, d, p, g).start()
            gc_copy(d, p, g).start()

    def relay(p):
        @pl.when(is_gate)
        def _():
            for i in range(mid):
                ag_wait(base_there + i, p)
                for j in range(1, mid):
                    ag_pass(i, j, p).start()
                spread_bins(base_there + i, p)

    def far_bins(p):
        @pl.when(jnp.logical_not(is_gate))
        def _():
            for i in range(mid):
                ag_wait(base_there + i, p)
                spread_bins(base_there + i, p)

    def near_bins(p):
        for j in range(1, mid):
            ag_wait(in_half(j), p)
            spread_bins(in_half(j), p)

    def pass_bins(p):
        for d in range(slabs):
            for j in range(1, chips):
                owner = ((chip - j) % chips) * 2 + core
                gx_copy(j, d, p, owner).wait_recv()
                gc_copy(d, p, owner).start()

    def core_bins():
        arrived(every_ref.at[:, 0 : chips * rows], gc_s.at[1])

    column = iota((here, LANES), 1)

    def backward(p):
        total = jnp.zeros((here, LANES), F32)
        for c in range(chunks):
            ticks = slice(c * block, (c + 1) * block)
            data = jnp.concatenate(
                [chalo_ref[0, p, :, ticks], cot_ref[p, :, ticks], chalo_ref[1, p, :, ticks]], 0
            )
            wide_ref[...] = dot(data, operator(p, c), ((1,), (1,)))
            low = jnp.zeros((here, LANES), F32)
            high = jnp.zeros((here, LANES), F32)
            for m in range(pairs):
                lanes = slice(m * LANES, (m + 1) * LANES)
                at = ROWS + half - 2 * m
                low += wide_ref[at : at + here, lanes]
                if 2 * m + 1 < spread:
                    high += wide_ref[at - 1 : at - 1 + here, lanes]
            first = block * c // TPB
            low = jnp.where(column < WIN, low, 0.0)
            high = jnp.where(column < WIN, 0.0, high)
            if first:
                low = pltpu.roll(low, first, 1)
            total += low + pltpu.roll(high, (WIN + first) % LANES, 1)
        every_ref[z, place_of(g, p), :] = total.astype(BF16)
        for j in range(mid):
            ag_copy(j, p).start()

    def sum_and_send(p):
        part = pl.ds(p * here, here)
        sums = own_ref[chip, part, :] + crecv_ref[chip, part, :].astype(F32)
        for j in range(1, chips):
            x_copy(j, p).wait_recv()
            sums += xrecv_ref[j - 1, p].astype(F32)
        frame(p, sums)
        send_windows(p)

    def window_sum(p):
        total = zsend_ref[z, p].astype(F32)
        for j in range(1, mid):
            half_copy(j, p).wait_recv()
            total += zrecv_ref[j - 1, p].astype(F32)
        sum_copy(0, p).wait_recv()
        total += zrecv_ref[mid - 1, p].astype(F32)
        field_ref[p, ROWS : ROWS + here, :] = total

    tall = here + 2 * ROWS
    used = tall

    def forward(p):
        window_sum(p)

        for side in range(2):

            @pl.when(has_prev if side == 0 else has_next)
            def _():
                arrived(hrecv_ref.at[side, :, p], h_r.at[side, p])

        for side, at in ((0, 0), (1, ROWS + here)):
            edge = hrecv_ref[side, 0, p].astype(F32)
            for j in range(1, mid + 1):
                edge += hrecv_ref[side, j, p].astype(F32)
            field_ref[p, at : at + ROWS, :] = edge
        for c in range(chunks):
            first = block * c // TPB
            this = field_ref[p, 0:used, :]
            following = field_ref[p, 1 : used + 1, :]
            if first:
                this = pltpu.roll(this, LANES - first, 1)
            following = pltpu.roll(following, (WIN - first) % LANES, 1)
            pair_ref[...] = jnp.where(iota((used, LANES), 1) < WIN, this, following)
            at = ROWS - half
            taken = [split(pair_ref[at + 2 * m : at + 2 * m + here, :]) for m in range(pairs)]
            upper, lower = (jnp.concatenate([t[n] for t in taken], 1) for n in range(2))
            both = dot(jnp.concatenate([upper, lower], 0), operator(p, c))
            total = both[:here] + both[here:] + dot(upper, operator(p, c, 1))
            sig_ref[p, :, c * block : (c + 1) * block] = total.astype(BF16)

    def windows_of(part):
        return jnp.concatenate([every_ref[d, part, :] for d in range(slabs)], 1)

    def shares(part, right):
        if turned:
            return dot(spread_t_ref[:, part], right)
        return dot(spread_ref[part, :], right, ((0,), (0,)))

    def grads(owner_core, extra):
        total = None
        for k in range(chips):
            part = pl.ds(pl.multiple_of((2 * k + owner_core) * rows, rows), rows)
            term = shares(part, windows_of(part))
            total = term if total is None else total + term
        if extra:
            part = slice(owners * rows, owners * rows + here)
            total += shares(part, windows_of(part))
        return total

    def merge(total):
        count = bins // LANES
        sums = [None] * count
        lanes = iota((blocks * cells, LANES), 1)
        for d in range(slabs):
            first = d * bins_here - front
            turn = first % LANES
            low = first // LANES
            window = total[:, d * LANES : (d + 1) * LANES]
            if turn:
                window = pltpu.roll(window, turn, 1)
            for n, keep in ((low, lanes >= turn), (low + 1, lanes < turn)):
                if 0 <= n < count:
                    piece = jnp.where(keep, window, 0.0)
                    sums[n] = piece if sums[n] is None else sums[n] + piece
        for n in range(count):
            grad_ref[:, n * LANES : (n + 1) * LANES] = sums[n].astype(BF16)

    def cot_edges():
        @pl.when(has_prev)
        def _():
            cot_up().wait_recv()

        @pl.when(has_next)
        def _():
            cot_down().wait_recv()

    def first_grads():
        total_ref[...] = grads(core, False)

    def last_grads():
        merge(total_ref[...] + grads(1 - core, True))

    def finish():
        for k in range(chips):
            core_copy(k).wait_send()
        if mid > 1:
            sent(zsend_ref.at[0 : mid - 1], z_s.at[0])
        sent(zsend_ref.at[0:mid], z_s.at[3])

        @pl.when(is_gate)
        def _():
            sent(zsend_ref.at[0:mid], z_s.at[2])
            for j in range(1, mid):
                sent(zsend_ref.at[0:mid], gr_s.at[j - 1])

        @pl.when(jnp.logical_not(is_gate))
        def _():
            sent(zsend_ref.at[0:mid], z_s.at[1])

        for side in range(2):

            @pl.when(edges(side))
            def _():
                sent(hrecv_ref.at[side, 0:mid], h_s.at[side])

            @pl.when(edges(side) & is_gate)
            def _():
                sent(hrecv_ref.at[side, 0:mid], h_s.at[2 + side])

        for j in range(1, chips):
            for p in range(2):
                x_copy(j, p).wait_send()
            sent(every_ref.at[:, 0:rows], gx_s.at[j - 1])
        sent(every_ref.at[:, 0 : chips * rows], gc_s.at[0])

        @pl.when(has_prev)
        def _():
            cot_down().wait_send()

        @pl.when(has_next)
        def _():
            cot_up().wait_send()

    green(0, 0)
    own_parts()
    core_sums()
    third_round()
    send_windows(2)
    green(1, 0)
    green(2, 0)
    loads[6].wait()
    cot_edges()
    backward(0)
    backward(1)
    all_here()
    gate_sums(2)
    core_copy(chip).wait_recv()
    sum_and_send(0)
    backward(2)
    relay(0)
    sum_and_send(1)
    spread_bins(z, 0)
    spread_bins(z, 1)
    relay(1)
    near_bins(0)
    near_bins(1)
    turn_shares()
    green(2, 1)
    gate_sums(0)
    green(0, 1)
    green(1, 1)
    gate_sums(1)
    relay(2)
    forward(2)
    far_bins(0)
    far_bins(1)
    pass_bins(0)
    forward(0)
    pass_bins(1)
    first_grads()
    forward(1)
    near_bins(2)
    far_bins(2)
    core_bins()
    last_grads()
    finish()


def store_kernel(signal_ref, grad_ref, signal_out, grad_out, sems):
    copies = (
        pltpu.make_async_copy(signal_ref, signal_out, sems.at[0]),
        pltpu.make_async_copy(grad_ref, grad_out, sems.at[1]),
    )
    for copy in copies:
        copy.start()
    for copy in copies:
        copy.wait()


def local(charge, intersection, ovl_block, ovl_count, diff_class, response, cotangent):
    blocks, planes, entries, wires, cells = intersection.shape
    bins = charge.shape[1]
    owners, slabs = lax.axis_size("gz"), lax.axis_size("drift")
    here, ticks_here = cotangent.shape[1:]
    spread, length = response.shape[1:]
    chips = owners // 2
    rows = 2 * here
    bins_here = bins // slabs
    block = math.gcd(ticks_here, 2 * LANES)
    pairs = (spread + 1) // 2
    front = (length - 1 + REACH + (TPB - 1) // 2) // TPB
    while (LOW - TPB * front) % LANES >= TPB:
        front += 1
    taps_rows = round_up(2 * pairs, 8)
    depth = round_up(length, ROWS)
    assert owners % 2 == 0 and slabs % 2 == 0 and planes == 3
    assert front + bins_here + HB <= LANES
    assert block * (ticks_here // block - 1) // TPB + WIN <= LANES
    assert length - 1 + REACH + (TPB - 1) // 2 - LOW < 2 * LANES
    dma = pltpu.SemaphoreType.DMA
    others = max(chips - 1, 1)
    mid = slabs // 2
    signal, charge_grad = pl.pallas_call(
        functools.partial(kernel, (owners, slabs, front, pairs, block)),
        out_shape=(
            jax.ShapeDtypeStruct((planes, here, ticks_here), BF16),
            jax.ShapeDtypeStruct((blocks * cells, bins), BF16),
        ),
        in_specs=[HBM] * 7,
        out_specs=(VMEM, VMEM),
        scratch_shapes=[
            pltpu.SMEM((planes, entries, blocks), jnp.int32),
            pltpu.SMEM(ovl_count.shape, jnp.int32),
            pltpu.VMEM(charge.shape, BF16),
            pltpu.VMEM(intersection.shape, BF16),
            pltpu.VMEM(diff_class.shape, jnp.int32),
            pltpu.VMEM(response.shape, BF16),
            pltpu.VMEM(cotangent.shape, BF16),
            dma((7,)),
            pltpu.SemaphoreType.REGULAR((2,)),
            pltpu.VMEM((owners * rows + here, blocks * cells), BF16),
            pltpu.VMEM((chips, rows, bins), F32),
            pltpu.VMEM((chips, rows, bins), BF16),
            pltpu.VMEM((chips, rows, bins), BF16),
            pltpu.VMEM((others, 2, here, bins), BF16),
            pltpu.VMEM((others, 2, here, bins), BF16),
            pltpu.VMEM((bins, slabs * LANES), BF16),
            pltpu.VMEM((slabs, planes, here, LANES), BF16),
            pltpu.VMEM((mid, planes, here, LANES), BF16),
            pltpu.VMEM((max(mid - 1, 1), mid, planes, here, LANES), BF16),
            pltpu.VMEM((mid, planes, here, LANES), BF16),
            pltpu.VMEM((2, mid + 1, planes, ROWS, LANES), BF16),
            pltpu.VMEM((2, planes, ROWS, ticks_here), BF16),
            pltpu.VMEM((slabs, owners * rows + here, LANES), BF16),
            pltpu.VMEM((blocks * cells, owners * rows + here), BF16),
            pltpu.VMEM((planes, taps_rows, depth), F32),
            pltpu.VMEM((2, planes * taps_rows * (NDIFF + 2), LANES), F32),
            pltpu.VMEM((2, planes, 2 * pairs, LANES, 4 * LANES), BF16),
            pltpu.VMEM((here + 2 * ROWS, 2 * pairs * WIN), F32),
            pltpu.VMEM((planes, here + 2 * ROWS + 8, LANES), F32),
            pltpu.VMEM((here + 2 * ROWS, LANES), F32),
            pltpu.VMEM((blocks * cells, slabs * LANES), F32),
            dma((chips,)),
            dma((chips,)),
            dma((others, 2)),
            dma((others, 2)),
            dma((4,)),
            dma((mid, planes)),
            dma((max(mid - 1, 1), planes)),
            dma((4,)),
            dma((2, planes)),
            dma((2,)),
            dma((2,)),
            dma((slabs, planes)),
            dma((max(mid - 1, 1),)),
            dma((others,)),
            dma((others, slabs, 2)),
            dma((2,)),
        ],
        compiler_params=pltpu.CompilerParams(
            collective_id=0, has_side_effects=True, vmem_limit_bytes=LIMIT * 1024 * 1024
        ),
        name="planes",
    )(
        *(
            pltpu.with_memory_space_constraint(array, pltpu.HBM)
            for array in (
                jnp.transpose(ovl_block, (1, 2, 0)),
                ovl_count,
                charge,
                intersection,
                diff_class,
                response,
                cotangent,
            )
        ),
    )
    return pl.pallas_call(
        store_kernel,
        out_shape=(
            jax.ShapeDtypeStruct(signal.shape, BF16),
            jax.ShapeDtypeStruct(charge_grad.shape, BF16),
        ),
        in_specs=[VMEM, VMEM],
        out_specs=(HBM, HBM),
        scratch_shapes=[pltpu.SemaphoreType.DMA((2,))],
        compiler_params=pltpu.CompilerParams(vmem_limit_bytes=4 * 1024 * 1024),
        name="store",
    )(signal, charge_grad)


def solution(mesh):
    return jax.shard_map(
        local,
        mesh=mesh,
        in_specs=(
            P(("apa", "gz", "drift"), None),
            P(("apa", "gz", "drift"), None, None, None, None),
            P(("apa", "gz", "drift"), None, None),
            P(("apa", "gz", "drift"), None),
            P("apa"),
            P(),
            P("apa", "gz", "drift"),
        ),
        out_specs=(P("apa", "gz", "drift"), P(("apa", "gz", "drift"), None)),
        check_vma=False,
    )
```

```python
import functools
import math

import jax
import jax.numpy as jnp
from jax import lax
from jax.experimental import pallas as pl
from jax.experimental.pallas import tpu as pltpu
from jax.sharding import PartitionSpec as P

TPB = 8
HB = 2
LIMIT = 44
LANES = 128
ROWS = 16
WIN = 64
NDIFF = 6
MESH = pl.DeviceIdType.MESH
F32 = jnp.float32
BF16 = jnp.bfloat16

VMEM = pl.BlockSpec(memory_space=pltpu.VMEM)
SMEM = pl.BlockSpec(memory_space=pltpu.SMEM)
HBM = pl.BlockSpec(memory_space=pltpu.HBM)

REACH = HB * TPB
LOW = -(REACH - (TPB - 1) // 2 - 1)


def round_up(value, step):
    return -(-value // step) * step


def iota(shape, dim):
    return lax.broadcasted_iota(jnp.int32, shape, dim)


def dot(left, right, contract=((1,), (0,))):
    return lax.dot_general(left, right, (contract, ((), ())), preferred_element_type=F32)


def class_scale(k):
    width = TPB * (0.2 + 0.15 * k)
    return 1.0 / (2.0 * width * width)


def class_norm(k):
    return sum(math.exp(-((j + 0.5) ** 2) * class_scale(k)) for j in range(-REACH, REACH))


def kernel(
    cfg,
    blk_hbm,
    cnt_hbm,
    charge_hbm,
    inter_hbm,
    class_hbm,
    resp_hbm,
    cot_hbm,
    sig_ref,
    grad_ref,
    blk_ref,
    cnt_ref,
    charge_ref,
    inter_ref,
    class_ref,
    resp_ref,
    cot_ref,
    load_s,
    round_s,
    spread_ref,
    own_ref,
    csend_ref,
    crecv_ref,
    xsend_ref,
    xrecv_ref,
    place_ref,
    zsend_ref,
    zrecv_ref,
    zgate_ref,
    zsum_ref,
    hrecv_ref,
    chalo_ref,
    every_ref,
    spread_t_ref,
    taps_ref,
    table_ref,
    green_ref,
    wide_ref,
    field_ref,
    pair_ref,
    total_ref,
    core_s,
    core_r,
    x_s,
    x_r,
    z_s,
    z_r,
    zg_r,
    h_s,
    h_r,
    c_s,
    c_r,
    ga_r,
    gr_s,
    gx_s,
    gx_r,
    gc_s,
):
    owners, slabs, front, pairs, block = cfg
    blocks, planes, entries, wires, cells = inter_ref.shape
    bins = charge_ref.shape[1]
    here, ticks_here = cot_ref.shape[1:]
    spread, length = resp_ref.shape[1:]
    per_owner = here // wires
    bins_here = bins // slabs
    half = (spread - 1) // 2
    chips = owners // 2
    rows = 2 * here
    chunks = ticks_here // block
    slots = 2 * pairs

    z = lax.axis_index("drift")
    g = lax.axis_index("gz")
    core = g % 2
    chip = g // 2
    partner = g + 1 - 2 * core

    def remote(src, dst, send, recv, gz, drift):
        return pltpu.make_async_remote_copy(
            src_ref=src,
            dst_ref=dst,
            send_sem=send,
            recv_sem=recv,
            device_id={"gz": gz, "drift": drift},
            device_id_type=MESH,
        )

    loads = [
        pltpu.make_async_copy(src, dst, load_s.at[n])
        for n, (src, dst) in enumerate(
            (
                (blk_hbm, blk_ref),
                (cnt_hbm, cnt_ref),
                (inter_hbm, inter_ref),
                (charge_hbm, charge_ref),
                (class_hbm, class_ref),
                (resp_hbm, resp_ref),
                (cot_hbm, cot_ref),
            )
        )
    ]
    for load in loads:
        load.start()

    barrier = pltpu.get_barrier_semaphore()

    def greet(sem, gz, drift):
        pl.semaphore_signal(
            sem, inc=1, device_id={"gz": gz, "drift": drift}, device_id_type=MESH
        )

    has_prev = g > 0
    has_next = g < owners - 1
    sides = has_prev.astype(jnp.int32) + has_next.astype(jnp.int32)
    has_left = z > 0
    has_right = z < slabs - 1
    rounds = chips == 2 and slabs <= 4

    def near(sem):
        for j in range(1, chips):
            greet(sem, ((chip + j) % chips) * 2 + core, z)
        if rounds:

            @pl.when(has_left)
            def _():
                greet(sem, g, z - 1)

            @pl.when(has_right)
            def _():
                greet(sem, g, z + 1)

        else:
            for j in range(1, slabs):
                greet(sem, g, (z + j) % slabs)
        here_only = [z] if rounds else list(range(slabs))

        @pl.when(has_prev)
        def _():
            for d in here_only:
                greet(sem, g - 1, d)

        @pl.when(has_next)
        def _():
            for d in here_only:
                greet(sem, g + 1, d)

    ends = has_left.astype(jnp.int32) + has_right.astype(jnp.int32)
    if rounds:
        near_count = (chips - 1) + ends + sides
    else:
        near_count = (chips - 1) + (slabs - 1) + slabs * sides
    near(barrier)

    def second_round():
        if rounds:
            near(round_s.at[0])

    def third_round():
        if rounds:
            pl.semaphore_wait(round_s.at[0], near_count)
            for step in (1, 2):

                @pl.when(z >= step)
                def _():
                    greet(round_s.at[1], g, z - step)

                @pl.when(z + step < slabs)
                def _():
                    greet(round_s.at[1], g, z + step)

    def all_here():
        if rounds:
            count = 0
            for step in (1, 2):
                count += (z >= step).astype(jnp.int32) + (z + step < slabs).astype(jnp.int32)
            pl.semaphore_wait(round_s.at[1], count)

    for load in loads[:3]:
        load.wait()
    def spread_block(block_index, p, at):
        for b in range(blocks):
            total = jnp.zeros((wires, cells), BF16)
            for k in range(entries):
                named = (blk_ref[p, k, b] == block_index) & (k < cnt_ref[b, p])
                total = total + jnp.where(named, inter_ref[b, p, k], jnp.zeros((wires, cells), BF16))
            spread_ref[pl.ds(at, wires), b * cells : (b + 1) * cells] = total

    def spread_owner(owner, _):
        for p in range(2):
            for q in range(per_owner):
                spread_block(
                    owner * per_owner + q,
                    p,
                    pl.multiple_of(owner * rows + (p * per_owner + q) * wires, wires),
                )
        return 0

    lax.fori_loop(0, owners, spread_owner, 0)
    for q in range(per_owner):
        spread_block(g * per_owner + q, 2, owners * rows + q * wires)

    loads[3].wait()
    charge = charge_ref[...]
    for k in range(chips):
        there = pl.multiple_of((2 * k + 1 - core) * rows, rows)
        csend_ref[k] = dot(spread_ref[pl.ds(there, rows), :], charge).astype(BF16)

    depth = round_up(length, ROWS)
    loads[4].wait()
    loads[5].wait()
    taps_ref[...] = jnp.zeros_like(taps_ref)
    for p in range(planes):
        taps_ref[p, 0:spread, 0:length] = resp_ref[p].astype(F32)
    taps = taps_ref[...].reshape(planes * taps_ref.shape[1], taps_ref.shape[2]).astype(BF16)
    row_class = class_ref[...].reshape(1, bins)
    tables = NDIFF + 2
    delta = iota((depth, 2 * LANES), 1) - iota((depth, 2 * LANES), 0)
    offset = (delta + LOW).astype(F32) - (TPB - 1) / 2
    inside = jnp.abs(offset) < REACH
    squared = offset * offset
    for k in range(tables):
        if k < NDIFF:
            scale, norm = class_scale(k), class_norm(k)
            keep = inside
        else:
            first = row_class[:, k - NDIFF : k - NDIFF + 1]
            scale = jnp.zeros((1, 1), F32)
            norm = jnp.zeros((1, 1), F32)
            for c in range(NDIFF):
                scale += jnp.where(first == c, class_scale(c), 0.0)
                norm += jnp.where(first == c, class_norm(c), 0.0)
            keep = inside & (delta + LOW + TPB * (k - NDIFF) >= 0)
        smear = jnp.where(keep, jnp.exp(-squared * scale), 0.0) / norm
        upper = smear.astype(BF16)
        lower = (smear - upper.astype(F32)).astype(BF16)
        spot = pl.ds(k, taps.shape[0], stride=tables)
        filtered = dot(taps, upper) + dot(taps, lower)
        table_ref[0, spot, :] = filtered[:, :LANES]
        table_ref[1, spot, :] = filtered[:, LANES:]

    bin_of = iota((LANES, bins), 0) + bins_here * z - front
    chosen = jnp.where(iota((LANES, bins), 1) == bin_of, 1.0, 0.0).astype(BF16)
    bin_row = iota((tables, bins), 1)
    table_row = iota((tables, bins), 0)
    wanted = jnp.where(bin_row < 2, NDIFF + bin_row, row_class)
    uses = jnp.where(table_row == wanted, 1.0, 0.0).astype(BF16)
    pick = dot(chosen, uses, ((1,), (1,))).astype(BF16)

    start = (LOW - TPB * front) % LANES
    blocks_of = LANES // TPB
    turn = iota((LANES, LANES), 0) % blocks_of * TPB + start
    right = iota((LANES, LANES), 1) >= turn
    group = slots // 2

    def split(value):
        upper = value.astype(BF16)
        return upper, (value - upper.astype(F32)).astype(BF16)

    def green_rows(p, part, step):
        j0 = step * group
        for u in range(group):
            j = j0 + u
            at = pl.multiple_of((p * taps_ref.shape[1] + j) * tables, tables)
            one, two = (
                pltpu.roll(
                    dot(pick, split(table_ref[n, pl.ds(at, tables), :])[part]),
                    start,
                    1,
                    stride=TPB,
                    stride_axis=0,
                )
                for n in range(2)
            )
            outs = (
                jnp.where(right, one, 0.0).astype(BF16),
                jnp.where(right, two, one).astype(BF16),
                jnp.where(right, 0.0, two).astype(BF16),
                jnp.zeros((LANES, LANES), BF16),
            )
            for q in range(LANES // blocks_of):
                here_rows = slice(q * blocks_of, (q + 1) * blocks_of)
                base = q - (TPB * front - LOW + start) // LANES
                for n in range(4):
                    lanes = (base + n) % 4 * LANES
                    green_ref[part, p, j, here_rows, lanes : lanes + LANES] = outs[n][here_rows]

    def green(p, part):
        def half_of(step, _):
            green_rows(p, part, step)
            return 0

        lax.fori_loop(0, 2, half_of, 0)

    def operator(p, c, half_of=0):
        first = block * c // TPB
        lanes = block * c % (4 * LANES)
        part = green_ref[half_of, p, :, first : first + WIN, lanes : lanes + block]
        return part.reshape(slots * WIN, block)

    pl.semaphore_wait(barrier, near_count)
    second_round()

    def core_copy(k):
        return remote(
            csend_ref.at[k], crecv_ref.at[k], core_s.at[k], core_r.at[k], partner, z
        )

    for j in range(1, chips + 1):
        core_copy((chip + j) % chips).start()

    def cot_down():
        return remote(
            cot_hbm.at[:, 0:ROWS], chalo_ref.at[1], c_s.at[1], c_r.at[1], g - 1, z
        )

    def cot_up():
        return remote(
            cot_hbm.at[:, here - ROWS : here], chalo_ref.at[0], c_s.at[0], c_r.at[0], g + 1, z
        )

    @pl.when(has_prev)
    def _():
        cot_down().start()

    @pl.when(has_next)
    def _():
        cot_up().start()

    @pl.when(g == 0)
    def _():
        chalo_ref[0] = jnp.zeros(chalo_ref.shape[1:], BF16)
        hrecv_ref[0] = jnp.zeros(hrecv_ref.shape[1:], BF16)

    @pl.when(g == owners - 1)
    def _():
        chalo_ref[1] = jnp.zeros(chalo_ref.shape[1:], BF16)
        hrecv_ref[1] = jnp.zeros(hrecv_ref.shape[1:], BF16)

    lane = iota((bins, slabs * LANES), 1)
    place_ref[...] = jnp.where(
        iota((bins, slabs * LANES), 0)
        == (lane // LANES) * bins_here - front + lane % LANES,
        1.0,
        0.0,
    ).astype(BF16)

    mid = slabs // 2
    low_half = z < mid
    base = jnp.where(low_half, 0, mid)
    base_there = mid - base
    gate = jnp.where(low_half, mid - 1, mid)
    gate_there = slabs - 1 - gate
    is_gate = z == gate

    def in_half(j):
        return base + (z - base + j) % mid

    def frame(p, sums):
        level = jnp.mean(sums, axis=1, keepdims=True).astype(BF16)
        framed = dot((sums - level.astype(F32)).astype(BF16), place_ref[...])
        for d in range(slabs):
            zsend_ref[d, p] = with_level(framed[:, d * LANES : (d + 1) * LANES], level)

    def with_level(window, upper, lower=0.0):
        at = iota(window.shape, 1)
        window = jnp.where(at == 0, upper.astype(F32), window)
        return jnp.where(at == 1, lower, window).astype(BF16)

    def level_of(window):
        return window[:, 0:1] + window[:, 1:2]

    def leveled(window):
        bin_here = iota(window.shape, 1) + bins_here * z - front
        known = (bin_here >= 0) & (bin_here < bins)
        return jnp.where(known, window + level_of(window), 0.0)

    def half_copy(j, p):
        return remote(
            zsend_ref.at[in_half(j), p],
            zrecv_ref.at[j - 1, p],
            z_s.at[0],
            z_r.at[j - 1, p],
            g,
            in_half(j),
        )

    giver = jnp.where(low_half, z, z - mid - 1)

    def gate_copy(i, p):
        return remote(
            zsend_ref.at[base_there + i, p],
            zgate_ref.at[jnp.clip(giver, 0, mid - 2), i, p],
            z_s.at[1],
            zg_r.at[jnp.clip(giver, 0, mid - 2), p],
            g,
            gate,
        )

    def arrived(ref, sem):
        remote(ref, ref, z_s.at[0], sem, g, z).wait_recv()

    def sent(ref, sem):
        remote(ref, ref, sem, z_r.at[0, 0], g, z).wait_send()

    def sum_copy(i, p):
        return remote(
            zsum_ref.at[i, p],
            zrecv_ref.at[mid - 1, p],
            z_s.at[2],
            z_r.at[mid - 1, p],
            g,
            base_there + i,
        )

    def edge_copy(side, j, p):
        rows_of = slice(here - ROWS, here) if side == 0 else slice(0, ROWS)
        return remote(
            zsend_ref.at[in_half(j), p, rows_of],
            hrecv_ref.at[side, j, p],
            h_s.at[side],
            h_r.at[side, p],
            g + 1 if side == 0 else g - 1,
            in_half(j),
        )

    def edge_sum(side, i, p):
        rows_of = slice(here - ROWS, here) if side == 0 else slice(0, ROWS)
        return remote(
            zsum_ref.at[i, p, rows_of],
            hrecv_ref.at[side, mid, p],
            h_s.at[2 + side],
            h_r.at[side, p],
            g + 1 if side == 0 else g - 1,
            base_there + i,
        )

    def edges(side):
        return has_next if side == 0 else has_prev

    def send_windows(p):
        @pl.when(jnp.logical_not(is_gate))
        def _():
            for i in range(mid):
                gate_copy(i, p).start()

        for j in range(1, mid):
            half_copy(j, p).start()
        for side in range(2):

            @pl.when(edges(side))
            def _():
                for j in range(mid):
                    edge_copy(side, j, p).start()

    def gate_sums(p):
        @pl.when(is_gate)
        def _():
            for n in range(mid - 1):
                arrived(zgate_ref.at[n, :, p], zg_r.at[n, p])
            for i in range(mid):
                total = zsend_ref[base_there + i, p].astype(F32)
                for n in range(mid - 1):
                    total += zgate_ref[n, i, p].astype(F32)
                level = level_of(total)
                upper = level.astype(BF16)
                zsum_ref[i, p] = with_level(total, upper, level - upper.astype(F32))
                sum_copy(i, p).start()
            for side in range(2):

                @pl.when(edges(side))
                def _():
                    for i in range(mid):
                        edge_sum(side, i, p).start()

    def own_parts():
        frame(2, dot(spread_ref[owners * rows : owners * rows + here, :], charge))
        for k in range(chips):
            there = pl.multiple_of((2 * k + core) * rows, rows)
            own_ref[k] = dot(spread_ref[pl.ds(there, rows), :], charge)

    turned = here % LANES == 0

    def turn_shares():
        if turned:
            for n in range(spread_ref.shape[0] // LANES):
                part = slice(n * LANES, (n + 1) * LANES)
                spread_t_ref[:, part] = spread_ref[part, :].T

    def x_copy(j, p):
        return remote(
            xsend_ref.at[j - 1, p],
            xrecv_ref.at[j - 1, p],
            x_s.at[j - 1, p],
            x_r.at[j - 1, p],
            ((chip + j) % chips) * 2 + core,
            z,
        )

    def core_sums():
        for j in range(1, chips):
            k = (chip + j) % chips
            core_copy(k).wait_recv()
            for p in range(2):
                part = pl.ds(p * here, here)
                xsend_ref[j - 1, p] = (
                    own_ref[k, part, :] + crecv_ref[k, part, :].astype(F32)
                ).astype(BF16)
                x_copy(j, p).start()

    def place_of(owner, p):
        at = owner * rows + p * here if p < 2 else owners * rows
        return pl.ds(pl.multiple_of(at, here), here)

    def block_at(d, owner, p):
        return every_ref.at[d, place_of(owner, p)]

    def ag_copy(j, p):
        part = block_at(z, g, p)
        to = in_half(j) if j else gate_there
        return remote(part, part, z_s.at[3], ga_r.at[z, p], g, to)

    def ag_pass(i, j, p):
        d = base_there + i
        part = block_at(d, g, p)
        return remote(part, part, gr_s.at[j - 1], ga_r.at[d, p], g, in_half(j))

    def ag_wait(d, p):
        part = block_at(d, g, p)
        arrived(part, ga_r.at[d, p])

    def gx_copy(j, d, p, owner):
        part = block_at(d, owner, p)
        return remote(
            part,
            part,
            gx_s.at[j - 1],
            gx_r.at[j - 1, d, p],
            ((chip + j) % chips) * 2 + core,
            z,
        )

    def gc_copy(d, p, owner):
        part = block_at(d, owner, p)
        return remote(part, part, gc_s.at[0], gc_s.at[1], partner, z)

    def spread_bins(d, p):
        if p < 2:
            for j in range(1, chips):
                gx_copy(j, d, p, g).start()
            gc_copy(d, p, g).start()

    def relay(p):
        @pl.when(is_gate)
        def _():
            for i in range(mid):
                ag_wait(base_there + i, p)
                for j in range(1, mid):
                    ag_pass(i, j, p).start()
                spread_bins(base_there + i, p)

    def far_bins(p):
        @pl.when(jnp.logical_not(is_gate))
        def _():
            for i in range(mid):
                ag_wait(base_there + i, p)
                spread_bins(base_there + i, p)

    def near_bins(p):
        for j in range(1, mid):
            ag_wait(in_half(j), p)
            spread_bins(in_half(j), p)

    def pass_bins(p):
        for d in range(slabs):
            for j in range(1, chips):
                owner = ((chip - j) % chips) * 2 + core
                gx_copy(j, d, p, owner).wait_recv()
                gc_copy(d, p, owner).start()

    def core_bins():
        arrived(every_ref.at[:, 0 : chips * rows], gc_s.at[1])

    column = iota((here, LANES), 1)

    def backward(p):
        total = jnp.zeros((here, LANES), F32)
        for c in range(chunks):
            ticks = slice(c * block, (c + 1) * block)
            data = jnp.concatenate(
                [chalo_ref[0, p, :, ticks], cot_ref[p, :, ticks], chalo_ref[1, p, :, ticks]], 0
            )
            wide_ref[...] = dot(data, operator(p, c), ((1,), (1,)))
            low = jnp.zeros((here, LANES), F32)
            high = jnp.zeros((here, LANES), F32)
            for m in range(pairs):
                lanes = slice(m * LANES, (m + 1) * LANES)
                at = ROWS + half - 2 * m
                low += wide_ref[at : at + here, lanes]
                if 2 * m + 1 < spread:
                    high += wide_ref[at - 1 : at - 1 + here, lanes]
            first = block * c // TPB
            low = jnp.where(column < WIN, low, 0.0)
            high = jnp.where(column < WIN, 0.0, high)
            if first:
                low = pltpu.roll(low, first, 1)
            total += low + pltpu.roll(high, (WIN + first) % LANES, 1)
        every_ref[z, place_of(g, p), :] = total.astype(BF16)
        for j in range(mid):
            ag_copy(j, p).start()

    def sum_and_send(p):
        part = pl.ds(p * here, here)
        sums = own_ref[chip, part, :] + crecv_ref[chip, part, :].astype(F32)
        for j in range(1, chips):
            x_copy(j, p).wait_recv()
            sums += xrecv_ref[j - 1, p].astype(F32)
        frame(p, sums)
        send_windows(p)

    def window_sum(p):
        total = zsend_ref[z, p].astype(F32)
        for j in range(1, mid):
            half_copy(j, p).wait_recv()
            total += zrecv_ref[j - 1, p].astype(F32)
        sum_copy(0, p).wait_recv()
        total += zrecv_ref[mid - 1, p].astype(F32)
        field_ref[p, ROWS : ROWS + here, :] = leveled(total)

    tall = here + 2 * ROWS
    used = tall

    def forward(p):
        window_sum(p)

        for side in range(2):

            @pl.when(has_prev if side == 0 else has_next)
            def _():
                arrived(hrecv_ref.at[side, :, p], h_r.at[side, p])

        for side, at in ((0, 0), (1, ROWS + here)):
            edge = hrecv_ref[side, 0, p].astype(F32)
            for j in range(1, mid + 1):
                edge += hrecv_ref[side, j, p].astype(F32)
            field_ref[p, at : at + ROWS, :] = leveled(edge)
        for c in range(chunks):
            first = block * c // TPB
            this = field_ref[p, 0:used, :]
            following = field_ref[p, 1 : used + 1, :]
            if first:
                this = pltpu.roll(this, LANES - first, 1)
            following = pltpu.roll(following, (WIN - first) % LANES, 1)
            pair_ref[...] = jnp.where(iota((used, LANES), 1) < WIN, this, following)
            at = ROWS - half
            taken = [split(pair_ref[at + 2 * m : at + 2 * m + here, :]) for m in range(pairs)]
            upper, lower = (jnp.concatenate([t[n] for t in taken], 1) for n in range(2))
            both = dot(jnp.concatenate([upper, lower], 0), operator(p, c))
            total = both[:here] + both[here:] + dot(upper, operator(p, c, 1))
            sig_ref[p, :, c * block : (c + 1) * block] = total.astype(BF16)

    def windows_of(part):
        return jnp.concatenate([every_ref[d, part, :] for d in range(slabs)], 1)

    def shares(part, right):
        if turned:
            return dot(spread_t_ref[:, part], right)
        return dot(spread_ref[part, :], right, ((0,), (0,)))

    def grads(owner_core, extra):
        total = None
        for k in range(chips):
            part = pl.ds(pl.multiple_of((2 * k + owner_core) * rows, rows), rows)
            term = shares(part, windows_of(part))
            total = term if total is None else total + term
        if extra:
            part = slice(owners * rows, owners * rows + here)
            total += shares(part, windows_of(part))
        return total

    def merge(total):
        count = bins // LANES
        sums = [None] * count
        lanes = iota((blocks * cells, LANES), 1)
        for d in range(slabs):
            first = d * bins_here - front
            turn = first % LANES
            low = first // LANES
            window = total[:, d * LANES : (d + 1) * LANES]
            if turn:
                window = pltpu.roll(window, turn, 1)
            for n, keep in ((low, lanes >= turn), (low + 1, lanes < turn)):
                if 0 <= n < count:
                    piece = jnp.where(keep, window, 0.0)
                    sums[n] = piece if sums[n] is None else sums[n] + piece
        for n in range(count):
            grad_ref[:, n * LANES : (n + 1) * LANES] = sums[n].astype(BF16)

    def cot_edges():
        @pl.when(has_prev)
        def _():
            cot_up().wait_recv()

        @pl.when(has_next)
        def _():
            cot_down().wait_recv()

    def first_grads():
        total_ref[...] = grads(core, False)

    def last_grads():
        merge(total_ref[...] + grads(1 - core, True))

    def finish():
        for k in range(chips):
            core_copy(k).wait_send()
        if mid > 1:
            sent(zsend_ref.at[0 : mid - 1], z_s.at[0])
        sent(zsend_ref.at[0:mid], z_s.at[3])

        @pl.when(is_gate)
        def _():
            sent(zsend_ref.at[0:mid], z_s.at[2])
            for j in range(1, mid):
                sent(zsend_ref.at[0:mid], gr_s.at[j - 1])

        @pl.when(jnp.logical_not(is_gate))
        def _():
            sent(zsend_ref.at[0:mid], z_s.at[1])

        for side in range(2):

            @pl.when(edges(side))
            def _():
                sent(hrecv_ref.at[side, 0:mid], h_s.at[side])

            @pl.when(edges(side) & is_gate)
            def _():
                sent(hrecv_ref.at[side, 0:mid], h_s.at[2 + side])

        for j in range(1, chips):
            for p in range(2):
                x_copy(j, p).wait_send()
            sent(every_ref.at[:, 0:rows], gx_s.at[j - 1])
        sent(every_ref.at[:, 0 : chips * rows], gc_s.at[0])

        @pl.when(has_prev)
        def _():
            cot_down().wait_send()

        @pl.when(has_next)
        def _():
            cot_up().wait_send()

    green(0, 0)
    own_parts()
    core_sums()
    third_round()
    send_windows(2)
    green(1, 0)
    green(2, 0)
    loads[6].wait()
    cot_edges()
    backward(0)
    backward(1)
    all_here()
    gate_sums(2)
    core_copy(chip).wait_recv()
    sum_and_send(0)
    backward(2)
    relay(0)
    sum_and_send(1)
    spread_bins(z, 0)
    spread_bins(z, 1)
    relay(1)
    near_bins(0)
    near_bins(1)
    turn_shares()
    green(2, 1)
    gate_sums(0)
    green(0, 1)
    green(1, 1)
    gate_sums(1)
    relay(2)
    forward(2)
    far_bins(0)
    far_bins(1)
    forward(0)
    pass_bins(0)
    pass_bins(1)
    first_grads()
    forward(1)
    near_bins(2)
    far_bins(2)
    core_bins()
    last_grads()
    finish()


def store_kernel(signal_ref, grad_ref, signal_out, grad_out, sems):
    copies = (
        pltpu.make_async_copy(signal_ref, signal_out, sems.at[0]),
        pltpu.make_async_copy(grad_ref, grad_out, sems.at[1]),
    )
    for copy in copies:
        copy.start()
    for copy in copies:
        copy.wait()


def local(charge, intersection, ovl_block, ovl_count, diff_class, response, cotangent):
    blocks, planes, entries, wires, cells = intersection.shape
    bins = charge.shape[1]
    owners, slabs = lax.axis_size("gz"), lax.axis_size("drift")
    here, ticks_here = cotangent.shape[1:]
    spread, length = response.shape[1:]
    chips = owners // 2
    rows = 2 * here
    bins_here = bins // slabs
    block = math.gcd(ticks_here, 2 * LANES)
    pairs = (spread + 1) // 2
    front = (length - 1 + REACH + (TPB - 1) // 2) // TPB
    least = front
    while (LOW - TPB * front) % LANES >= TPB:
        front += 1
    taps_rows = round_up(2 * pairs, 8)
    depth = round_up(length, ROWS)
    assert owners % 2 == 0 and slabs % 2 == 0 and planes == 3
    assert front - least >= 2 and front + bins_here + HB <= LANES
    assert block * (ticks_here // block - 1) // TPB + WIN <= LANES
    assert length - 1 + REACH + (TPB - 1) // 2 - LOW < 2 * LANES
    dma = pltpu.SemaphoreType.DMA
    others = max(chips - 1, 1)
    mid = slabs // 2
    signal, charge_grad = pl.pallas_call(
        functools.partial(kernel, (owners, slabs, front, pairs, block)),
        out_shape=(
            jax.ShapeDtypeStruct((planes, here, ticks_here), BF16),
            jax.ShapeDtypeStruct((blocks * cells, bins), BF16),
        ),
        in_specs=[HBM] * 7,
        out_specs=(VMEM, VMEM),
        scratch_shapes=[
            pltpu.SMEM((planes, entries, blocks), jnp.int32),
            pltpu.SMEM(ovl_count.shape, jnp.int32),
            pltpu.VMEM(charge.shape, BF16),
            pltpu.VMEM(intersection.shape, BF16),
            pltpu.VMEM(diff_class.shape, jnp.int32),
            pltpu.VMEM(response.shape, BF16),
            pltpu.VMEM(cotangent.shape, BF16),
            dma((7,)),
            pltpu.SemaphoreType.REGULAR((2,)),
            pltpu.VMEM((owners * rows + here, blocks * cells), BF16),
            pltpu.VMEM((chips, rows, bins), F32),
            pltpu.VMEM((chips, rows, bins), BF16),
            pltpu.VMEM((chips, rows, bins), BF16),
            pltpu.VMEM((others, 2, here, bins), BF16),
            pltpu.VMEM((others, 2, here, bins), BF16),
            pltpu.VMEM((bins, slabs * LANES), BF16),
            pltpu.VMEM((slabs, planes, here, LANES), BF16),
            pltpu.VMEM((mid, planes, here, LANES), BF16),
            pltpu.VMEM((max(mid - 1, 1), mid, planes, here, LANES), BF16),
            pltpu.VMEM((mid, planes, here, LANES), BF16),
            pltpu.VMEM((2, mid + 1, planes, ROWS, LANES), BF16),
            pltpu.VMEM((2, planes, ROWS, ticks_here), BF16),
            pltpu.VMEM((slabs, owners * rows + here, LANES), BF16),
            pltpu.VMEM((blocks * cells, owners * rows + here), BF16),
            pltpu.VMEM((planes, taps_rows, depth), F32),
            pltpu.VMEM((2, planes * taps_rows * (NDIFF + 2), LANES), F32),
            pltpu.VMEM((2, planes, 2 * pairs, LANES, 4 * LANES), BF16),
            pltpu.VMEM((here + 2 * ROWS, 2 * pairs * WIN), F32),
            pltpu.VMEM((planes, here + 2 * ROWS + 8, LANES), F32),
            pltpu.VMEM((here + 2 * ROWS, LANES), F32),
            pltpu.VMEM((blocks * cells, slabs * LANES), F32),
            dma((chips,)),
            dma((chips,)),
            dma((others, 2)),
            dma((others, 2)),
            dma((4,)),
            dma((mid, planes)),
            dma((max(mid - 1, 1), planes)),
            dma((4,)),
            dma((2, planes)),
            dma((2,)),
            dma((2,)),
            dma((slabs, planes)),
            dma((max(mid - 1, 1),)),
            dma((others,)),
            dma((others, slabs, 2)),
            dma((2,)),
        ],
        compiler_params=pltpu.CompilerParams(
            collective_id=0, has_side_effects=True, vmem_limit_bytes=LIMIT * 1024 * 1024
        ),
        name="planes",
    )(
        *(
            pltpu.with_memory_space_constraint(array, pltpu.HBM)
            for array in (
                jnp.transpose(ovl_block, (1, 2, 0)),
                ovl_count,
                charge,
                intersection,
                diff_class,
                response,
                cotangent,
            )
        ),
    )
    return pl.pallas_call(
        store_kernel,
        out_shape=(
            jax.ShapeDtypeStruct(signal.shape, BF16),
            jax.ShapeDtypeStruct(charge_grad.shape, BF16),
        ),
        in_specs=[VMEM, VMEM],
        out_specs=(HBM, HBM),
        scratch_shapes=[pltpu.SemaphoreType.DMA((2,))],
        compiler_params=pltpu.CompilerParams(vmem_limit_bytes=4 * 1024 * 1024),
        name="store",
    )(signal, charge_grad)


def solution(mesh):
    return jax.shard_map(
        local,
        mesh=mesh,
        in_specs=(
            P(("apa", "gz", "drift"), None),
            P(("apa", "gz", "drift"), None, None, None, None),
            P(("apa", "gz", "drift"), None, None),
            P(("apa", "gz", "drift"), None),
            P("apa"),
            P(),
            P("apa", "gz", "drift"),
        ),
        out_specs=(P("apa", "gz", "drift"), P(("apa", "gz", "drift"), None)),
        check_vma=False,
    )
```

```python
import functools
import math

import jax
import jax.numpy as jnp
from jax import lax
from jax.experimental import pallas as pl
from jax.experimental.pallas import tpu as pltpu
from jax.sharding import PartitionSpec as P

TPB = 8
HB = 2
LIMIT = 44
LANES = 128
ROWS = 16
WIN = 64
NDIFF = 6
MESH = pl.DeviceIdType.MESH
F32 = jnp.float32
BF16 = jnp.bfloat16

VMEM = pl.BlockSpec(memory_space=pltpu.VMEM)
SMEM = pl.BlockSpec(memory_space=pltpu.SMEM)
HBM = pl.BlockSpec(memory_space=pltpu.HBM)

REACH = HB * TPB
LOW = -(REACH - (TPB - 1) // 2 - 1)


def round_up(value, step):
    return -(-value // step) * step


def iota(shape, dim):
    return lax.broadcasted_iota(jnp.int32, shape, dim)


def dot(left, right, contract=((1,), (0,))):
    return lax.dot_general(left, right, (contract, ((), ())), preferred_element_type=F32)


def class_scale(k):
    width = TPB * (0.2 + 0.15 * k)
    return 1.0 / (2.0 * width * width)


def class_norm(k):
    return sum(math.exp(-((j + 0.5) ** 2) * class_scale(k)) for j in range(-REACH, REACH))


def kernel(
    cfg,
    blk_hbm,
    cnt_hbm,
    charge_hbm,
    inter_hbm,
    class_hbm,
    resp_hbm,
    cot_hbm,
    sig_ref,
    grad_ref,
    blk_ref,
    cnt_ref,
    charge_ref,
    inter_ref,
    class_ref,
    resp_ref,
    cot_ref,
    load_s,
    round_s,
    spread_ref,
    own_ref,
    csend_ref,
    crecv_ref,
    xsend_ref,
    xrecv_ref,
    place_ref,
    zsend_ref,
    zrecv_ref,
    zgate_ref,
    zsum_ref,
    hrecv_ref,
    chalo_ref,
    every_ref,
    spread_t_ref,
    taps_ref,
    table_ref,
    green_ref,
    wide_ref,
    field_ref,
    pair_ref,
    total_ref,
    core_s,
    core_r,
    x_s,
    x_r,
    z_s,
    z_r,
    zg_r,
    h_s,
    h_r,
    c_s,
    c_r,
    ga_r,
    gr_s,
    gx_s,
    gx_r,
    gc_s,
):
    owners, slabs, front, pairs, block = cfg
    blocks, planes, entries, wires, cells = inter_ref.shape
    bins = charge_ref.shape[1]
    here, ticks_here = cot_ref.shape[1:]
    spread, length = resp_ref.shape[1:]
    per_owner = here // wires
    bins_here = bins // slabs
    half = (spread - 1) // 2
    chips = owners // 2
    rows = 2 * here
    chunks = ticks_here // block
    slots = 2 * pairs

    z = lax.axis_index("drift")
    g = lax.axis_index("gz")
    core = g % 2
    chip = g // 2
    partner = g + 1 - 2 * core

    def remote(src, dst, send, recv, gz, drift):
        return pltpu.make_async_remote_copy(
            src_ref=src,
            dst_ref=dst,
            send_sem=send,
            recv_sem=recv,
            device_id={"gz": gz, "drift": drift},
            device_id_type=MESH,
        )

    loads = [
        pltpu.make_async_copy(src, dst, load_s.at[n])
        for n, (src, dst) in enumerate(
            (
                (blk_hbm, blk_ref),
                (cnt_hbm, cnt_ref),
                (inter_hbm, inter_ref),
                (charge_hbm, charge_ref),
                (class_hbm, class_ref),
                (resp_hbm, resp_ref),
                (cot_hbm, cot_ref),
            )
        )
    ]
    for load in loads:
        load.start()

    barrier = pltpu.get_barrier_semaphore()

    def greet(sem, gz, drift):
        pl.semaphore_signal(
            sem, inc=1, device_id={"gz": gz, "drift": drift}, device_id_type=MESH
        )

    has_prev = g > 0
    has_next = g < owners - 1
    sides = has_prev.astype(jnp.int32) + has_next.astype(jnp.int32)
    has_left = z > 0
    has_right = z < slabs - 1
    rounds = chips == 2 and slabs <= 4

    def near(sem):
        for j in range(1, chips):
            greet(sem, ((chip + j) % chips) * 2 + core, z)
        if rounds:

            @pl.when(has_left)
            def _():
                greet(sem, g, z - 1)

            @pl.when(has_right)
            def _():
                greet(sem, g, z + 1)

        else:
            for j in range(1, slabs):
                greet(sem, g, (z + j) % slabs)
        here_only = [z] if rounds else list(range(slabs))

        @pl.when(has_prev)
        def _():
            for d in here_only:
                greet(sem, g - 1, d)

        @pl.when(has_next)
        def _():
            for d in here_only:
                greet(sem, g + 1, d)

    ends = has_left.astype(jnp.int32) + has_right.astype(jnp.int32)
    if rounds:
        near_count = (chips - 1) + ends + sides
    else:
        near_count = (chips - 1) + (slabs - 1) + slabs * sides
    near(barrier)

    def second_round():
        if rounds:
            near(round_s.at[0])

    def third_round():
        if rounds:
            pl.semaphore_wait(round_s.at[0], near_count)
            for step in (1, 2):

                @pl.when(z >= step)
                def _():
                    greet(round_s.at[1], g, z - step)

                @pl.when(z + step < slabs)
                def _():
                    greet(round_s.at[1], g, z + step)

    def all_here():
        if rounds:
            count = 0
            for step in (1, 2):
                count += (z >= step).astype(jnp.int32) + (z + step < slabs).astype(jnp.int32)
            pl.semaphore_wait(round_s.at[1], count)

    for load in loads[:3]:
        load.wait()
    def spread_block(block_index, p, at):
        for b in range(blocks):
            total = jnp.zeros((wires, cells), BF16)
            for k in range(entries):
                named = (blk_ref[p, k, b] == block_index) & (k < cnt_ref[b, p])
                total = total + jnp.where(named, inter_ref[b, p, k], jnp.zeros((wires, cells), BF16))
            spread_ref[pl.ds(at, wires), b * cells : (b + 1) * cells] = total

    def spread_owner(owner, _):
        for p in range(2):
            for q in range(per_owner):
                spread_block(
                    owner * per_owner + q,
                    p,
                    pl.multiple_of(owner * rows + (p * per_owner + q) * wires, wires),
                )
        return 0

    lax.fori_loop(0, owners, spread_owner, 0)
    for q in range(per_owner):
        spread_block(g * per_owner + q, 2, owners * rows + q * wires)

    loads[3].wait()
    charge = charge_ref[...]
    for k in range(chips):
        there = pl.multiple_of((2 * k + 1 - core) * rows, rows)
        csend_ref[k] = dot(spread_ref[pl.ds(there, rows), :], charge).astype(BF16)

    depth = round_up(length, ROWS)
    loads[4].wait()
    loads[5].wait()
    taps_ref[...] = jnp.zeros_like(taps_ref)
    for p in range(planes):
        taps_ref[p, 0:spread, 0:length] = resp_ref[p].astype(F32)
    taps = taps_ref[...].reshape(planes * taps_ref.shape[1], taps_ref.shape[2]).astype(BF16)
    row_class = class_ref[...].reshape(1, bins)
    tables = NDIFF + 2
    delta = iota((depth, 2 * LANES), 1) - iota((depth, 2 * LANES), 0)
    offset = (delta + LOW).astype(F32) - (TPB - 1) / 2
    inside = jnp.abs(offset) < REACH
    squared = offset * offset
    for k in range(tables):
        if k < NDIFF:
            scale, norm = class_scale(k), class_norm(k)
            keep = inside
        else:
            first = row_class[:, k - NDIFF : k - NDIFF + 1]
            scale = jnp.zeros((1, 1), F32)
            norm = jnp.zeros((1, 1), F32)
            for c in range(NDIFF):
                scale += jnp.where(first == c, class_scale(c), 0.0)
                norm += jnp.where(first == c, class_norm(c), 0.0)
            keep = inside & (delta + LOW + TPB * (k - NDIFF) >= 0)
        smear = jnp.where(keep, jnp.exp(-squared * scale), 0.0) / norm
        upper = smear.astype(BF16)
        lower = (smear - upper.astype(F32)).astype(BF16)
        spot = pl.ds(k, taps.shape[0], stride=tables)
        filtered = dot(taps, upper) + dot(taps, lower)
        table_ref[0, spot, :] = filtered[:, :LANES]
        table_ref[1, spot, :] = filtered[:, LANES:]

    bin_of = iota((LANES, bins), 0) + bins_here * z - front
    chosen = jnp.where(iota((LANES, bins), 1) == bin_of, 1.0, 0.0).astype(BF16)
    bin_row = iota((tables, bins), 1)
    table_row = iota((tables, bins), 0)
    wanted = jnp.where(bin_row < 2, NDIFF + bin_row, row_class)
    uses = jnp.where(table_row == wanted, 1.0, 0.0).astype(BF16)
    pick = dot(chosen, uses, ((1,), (1,))).astype(BF16)

    start = (LOW - TPB * front) % LANES
    blocks_of = LANES // TPB
    turn = iota((LANES, LANES), 0) % blocks_of * TPB + start
    right = iota((LANES, LANES), 1) >= turn
    group = slots // 2

    def split(value):
        upper = value.astype(BF16)
        return upper, (value - upper.astype(F32)).astype(BF16)

    def green_rows(p, part, step):
        j0 = step * group
        for u in range(group):
            j = j0 + u
            at = pl.multiple_of((p * taps_ref.shape[1] + j) * tables, tables)
            one, two = (
                pltpu.roll(
                    dot(pick, split(table_ref[n, pl.ds(at, tables), :])[part]),
                    start,
                    1,
                    stride=TPB,
                    stride_axis=0,
                )
                for n in range(2)
            )
            outs = (
                jnp.where(right, one, 0.0).astype(BF16),
                jnp.where(right, two, one).astype(BF16),
                jnp.where(right, 0.0, two).astype(BF16),
                jnp.zeros((LANES, LANES), BF16),
            )
            for q in range(LANES // blocks_of):
                here_rows = slice(q * blocks_of, (q + 1) * blocks_of)
                base = q - (TPB * front - LOW + start) // LANES
                for n in range(4):
                    lanes = (base + n) % 4 * LANES
                    green_ref[part, p, j, here_rows, lanes : lanes + LANES] = outs[n][here_rows]

    def green(p, part):
        def half_of(step, _):
            green_rows(p, part, step)
            return 0

        lax.fori_loop(0, 2, half_of, 0)

    def operator(p, c, half_of=0):
        first = block * c // TPB
        lanes = block * c % (4 * LANES)
        part = green_ref[half_of, p, :, first : first + WIN, lanes : lanes + block]
        return part.reshape(slots * WIN, block)

    pl.semaphore_wait(barrier, near_count)
    second_round()

    def core_copy(k):
        return remote(
            csend_ref.at[k], crecv_ref.at[k], core_s.at[k], core_r.at[k], partner, z
        )

    for j in range(1, chips + 1):
        core_copy((chip + j) % chips).start()

    def cot_down():
        return remote(
            cot_hbm.at[:, 0:ROWS], chalo_ref.at[1], c_s.at[1], c_r.at[1], g - 1, z
        )

    def cot_up():
        return remote(
            cot_hbm.at[:, here - ROWS : here], chalo_ref.at[0], c_s.at[0], c_r.at[0], g + 1, z
        )

    @pl.when(has_prev)
    def _():
        cot_down().start()

    @pl.when(has_next)
    def _():
        cot_up().start()

    @pl.when(g == 0)
    def _():
        chalo_ref[0] = jnp.zeros(chalo_ref.shape[1:], BF16)
        hrecv_ref[0] = jnp.zeros(hrecv_ref.shape[1:], BF16)

    @pl.when(g == owners - 1)
    def _():
        chalo_ref[1] = jnp.zeros(chalo_ref.shape[1:], BF16)
        hrecv_ref[1] = jnp.zeros(hrecv_ref.shape[1:], BF16)

    lane = iota((bins, slabs * LANES), 1)
    place_ref[...] = jnp.where(
        iota((bins, slabs * LANES), 0)
        == (lane // LANES) * bins_here - front + lane % LANES,
        1.0,
        0.0,
    ).astype(BF16)

    mid = slabs // 2
    low_half = z < mid
    base = jnp.where(low_half, 0, mid)
    base_there = mid - base
    gate = jnp.where(low_half, mid - 1, mid)
    gate_there = slabs - 1 - gate
    is_gate = z == gate

    def in_half(j):
        return base + (z - base + j) % mid

    def frame(p, sums):
        level = jnp.mean(sums, axis=1, keepdims=True).astype(BF16)
        framed = dot((sums - level.astype(F32)).astype(BF16), place_ref[...])
        for d in range(slabs):
            zsend_ref[d, p] = with_level(framed[:, d * LANES : (d + 1) * LANES], level)

    def with_level(window, upper, lower=0.0):
        at = iota(window.shape, 1)
        window = jnp.where(at == 0, upper.astype(F32), window)
        return jnp.where(at == 1, lower, window).astype(BF16)

    def level_of(window):
        return window[:, 0:1] + window[:, 1:2]

    def leveled(window):
        bin_here = iota(window.shape, 1) + bins_here * z - front
        known = (bin_here >= 0) & (bin_here < bins)
        return jnp.where(known, window + level_of(window), 0.0)

    def half_copy(j, p):
        return remote(
            zsend_ref.at[in_half(j), p],
            zrecv_ref.at[j - 1, p],
            z_s.at[0],
            z_r.at[j - 1, p],
            g,
            in_half(j),
        )

    giver = jnp.where(low_half, z, z - mid - 1)

    def gate_copy(i, p):
        return remote(
            zsend_ref.at[base_there + i, p],
            zgate_ref.at[jnp.clip(giver, 0, mid - 2), i, p],
            z_s.at[1],
            zg_r.at[jnp.clip(giver, 0, mid - 2), p],
            g,
            gate,
        )

    def arrived(ref, sem):
        remote(ref, ref, z_s.at[0], sem, g, z).wait_recv()

    def sent(ref, sem):
        remote(ref, ref, sem, z_r.at[0, 0], g, z).wait_send()

    def sum_copy(i, p):
        return remote(
            zsum_ref.at[i, p],
            zrecv_ref.at[mid - 1, p],
            z_s.at[2],
            z_r.at[mid - 1, p],
            g,
            base_there + i,
        )

    def edge_copy(side, j, p):
        rows_of = slice(here - ROWS, here) if side == 0 else slice(0, ROWS)
        return remote(
            zsend_ref.at[in_half(j), p, rows_of],
            hrecv_ref.at[side, j, p],
            h_s.at[side],
            h_r.at[side, p],
            g + 1 if side == 0 else g - 1,
            in_half(j),
        )

    def edge_sum(side, i, p):
        rows_of = slice(here - ROWS, here) if side == 0 else slice(0, ROWS)
        return remote(
            zsum_ref.at[i, p, rows_of],
            hrecv_ref.at[side, mid, p],
            h_s.at[2 + side],
            h_r.at[side, p],
            g + 1 if side == 0 else g - 1,
            base_there + i,
        )

    def edges(side):
        return has_next if side == 0 else has_prev

    def send_windows(p):
        @pl.when(jnp.logical_not(is_gate))
        def _():
            for i in range(mid):
                gate_copy(i, p).start()

        for j in range(1, mid):
            half_copy(j, p).start()
        for side in range(2):

            @pl.when(edges(side))
            def _():
                for j in range(mid):
                    edge_copy(side, j, p).start()

    def gate_sums(p):
        @pl.when(is_gate)
        def _():
            for n in range(mid - 1):
                arrived(zgate_ref.at[n, :, p], zg_r.at[n, p])
            for i in range(mid):
                total = zsend_ref[base_there + i, p].astype(F32)
                for n in range(mid - 1):
                    total += zgate_ref[n, i, p].astype(F32)
                level = level_of(total)
                upper = level.astype(BF16)
                zsum_ref[i, p] = with_level(total, upper, level - upper.astype(F32))
                sum_copy(i, p).start()
            for side in range(2):

                @pl.when(edges(side))
                def _():
                    for i in range(mid):
                        edge_sum(side, i, p).start()

    def own_parts():
        frame(2, dot(spread_ref[owners * rows : owners * rows + here, :], charge))
        for k in range(chips):
            there = pl.multiple_of((2 * k + core) * rows, rows)
            own_ref[k] = dot(spread_ref[pl.ds(there, rows), :], charge)

    turned = here % LANES == 0

    def turn_shares():
        if turned:
            for n in range(spread_ref.shape[0] // LANES):
                part = slice(n * LANES, (n + 1) * LANES)
                spread_t_ref[:, part] = spread_ref[part, :].T

    def x_copy(j, p):
        return remote(
            xsend_ref.at[j - 1, p],
            xrecv_ref.at[j - 1, p],
            x_s.at[j - 1, p],
            x_r.at[j - 1, p],
            ((chip + j) % chips) * 2 + core,
            z,
        )

    def core_sums():
        for j in range(1, chips):
            k = (chip + j) % chips
            core_copy(k).wait_recv()
            for p in range(2):
                part = pl.ds(p * here, here)
                xsend_ref[j - 1, p] = (
                    own_ref[k, part, :] + crecv_ref[k, part, :].astype(F32)
                ).astype(BF16)
                x_copy(j, p).start()

    def place_of(owner, p):
        at = owner * rows + p * here if p < 2 else owners * rows
        return pl.ds(pl.multiple_of(at, here), here)

    def block_at(d, owner, p):
        return every_ref.at[d, place_of(owner, p)]

    def ag_copy(j, p):
        part = block_at(z, g, p)
        to = in_half(j) if j else gate_there
        return remote(part, part, z_s.at[3], ga_r.at[z, p], g, to)

    def ag_pass(i, j, p):
        d = base_there + i
        part = block_at(d, g, p)
        return remote(part, part, gr_s.at[j - 1], ga_r.at[d, p], g, in_half(j))

    def ag_wait(d, p):
        part = block_at(d, g, p)
        arrived(part, ga_r.at[d, p])

    def gx_copy(j, d, p, owner):
        part = block_at(d, owner, p)
        return remote(
            part,
            part,
            gx_s.at[j - 1],
            gx_r.at[j - 1, d, p],
            ((chip + j) % chips) * 2 + core,
            z,
        )

    def gc_copy(d, p, owner):
        part = block_at(d, owner, p)
        return remote(part, part, gc_s.at[0], gc_s.at[1], partner, z)

    def spread_bins(d, p):
        if p < 2:
            for j in range(1, chips):
                gx_copy(j, d, p, g).start()
            gc_copy(d, p, g).start()

    def relay(p):
        @pl.when(is_gate)
        def _():
            for i in range(mid):
                ag_wait(base_there + i, p)
                for j in range(1, mid):
                    ag_pass(i, j, p).start()
                spread_bins(base_there + i, p)

    def far_bins(p):
        @pl.when(jnp.logical_not(is_gate))
        def _():
            for i in range(mid):
                ag_wait(base_there + i, p)
                spread_bins(base_there + i, p)

    def near_bins(p):
        for j in range(1, mid):
            ag_wait(in_half(j), p)
            spread_bins(in_half(j), p)

    def pass_bins(p):
        for d in range(slabs):
            for j in range(1, chips):
                owner = ((chip - j) % chips) * 2 + core
                gx_copy(j, d, p, owner).wait_recv()
                gc_copy(d, p, owner).start()

    def core_bins():
        arrived(every_ref.at[:, 0 : chips * rows], gc_s.at[1])

    column = iota((here, LANES), 1)

    def backward(p):
        total = jnp.zeros((here, LANES), F32)
        for c in range(chunks):
            ticks = slice(c * block, (c + 1) * block)
            data = jnp.concatenate(
                [chalo_ref[0, p, :, ticks], cot_ref[p, :, ticks], chalo_ref[1, p, :, ticks]], 0
            )
            wide_ref[...] = dot(data, operator(p, c), ((1,), (1,)))
            low = jnp.zeros((here, LANES), F32)
            high = jnp.zeros((here, LANES), F32)
            for m in range(pairs):
                lanes = slice(m * LANES, (m + 1) * LANES)
                at = ROWS + half - 2 * m
                low += wide_ref[at : at + here, lanes]
                if 2 * m + 1 < spread:
                    high += wide_ref[at - 1 : at - 1 + here, lanes]
            first = block * c // TPB
            low = jnp.where(column < WIN, low, 0.0)
            high = jnp.where(column < WIN, 0.0, high)
            if first:
                low = pltpu.roll(low, first, 1)
            total += low + pltpu.roll(high, (WIN + first) % LANES, 1)
        every_ref[z, place_of(g, p), :] = total.astype(BF16)
        for j in range(mid):
            ag_copy(j, p).start()

    def sum_and_send(p):
        part = pl.ds(p * here, here)
        sums = own_ref[chip, part, :] + crecv_ref[chip, part, :].astype(F32)
        for j in range(1, chips):
            x_copy(j, p).wait_recv()
            sums += xrecv_ref[j - 1, p].astype(F32)
        frame(p, sums)
        send_windows(p)

    def window_sum(p):
        total = zsend_ref[z, p].astype(F32)
        for j in range(1, mid):
            half_copy(j, p).wait_recv()
            total += zrecv_ref[j - 1, p].astype(F32)
        sum_copy(0, p).wait_recv()
        total += zrecv_ref[mid - 1, p].astype(F32)
        field_ref[p, ROWS : ROWS + here, :] = leveled(total)

    tall = here + 2 * ROWS
    used = tall

    def forward(p):
        window_sum(p)

        for side in range(2):

            @pl.when(has_prev if side == 0 else has_next)
            def _():
                arrived(hrecv_ref.at[side, :, p], h_r.at[side, p])

        for side, at in ((0, 0), (1, ROWS + here)):
            edge = hrecv_ref[side, 0, p].astype(F32)
            for j in range(1, mid + 1):
                edge += hrecv_ref[side, j, p].astype(F32)
            field_ref[p, at : at + ROWS, :] = leveled(edge)
        for c in range(chunks):
            first = block * c // TPB
            this = field_ref[p, 0:used, :]
            following = field_ref[p, 1 : used + 1, :]
            if first:
                this = pltpu.roll(this, LANES - first, 1)
            following = pltpu.roll(following, (WIN - first) % LANES, 1)
            pair_ref[...] = jnp.where(iota((used, LANES), 1) < WIN, this, following)
            at = ROWS - half
            taken = [split(pair_ref[at + 2 * m : at + 2 * m + here, :]) for m in range(pairs)]
            upper, lower = (jnp.concatenate([t[n] for t in taken], 1) for n in range(2))
            both = dot(jnp.concatenate([upper, lower], 0), operator(p, c))
            total = both[:here] + both[here:] + dot(upper, operator(p, c, 1))
            sig_ref[p, :, c * block : (c + 1) * block] = total.astype(BF16)

    def windows_of(part):
        return jnp.concatenate([every_ref[d, part, :] for d in range(slabs)], 1)

    def shares(part, right):
        if turned:
            return dot(spread_t_ref[:, part], right)
        return dot(spread_ref[part, :], right, ((0,), (0,)))

    def grads(owner_core, extra):
        total = None
        for k in range(chips):
            part = pl.ds(pl.multiple_of((2 * k + owner_core) * rows, rows), rows)
            term = shares(part, windows_of(part))
            total = term if total is None else total + term
        if extra:
            part = slice(owners * rows, owners * rows + here)
            total += shares(part, windows_of(part))
        return total

    def merge(total):
        count = bins // LANES
        sums = [None] * count
        lanes = iota((blocks * cells, LANES), 1)
        for d in range(slabs):
            first = d * bins_here - front
            turn = first % LANES
            low = first // LANES
            window = total[:, d * LANES : (d + 1) * LANES]
            if turn:
                window = pltpu.roll(window, turn, 1)
            for n, keep in ((low, lanes >= turn), (low + 1, lanes < turn)):
                if 0 <= n < count:
                    piece = jnp.where(keep, window, 0.0)
                    sums[n] = piece if sums[n] is None else sums[n] + piece
        for n in range(count):
            grad_ref[:, n * LANES : (n + 1) * LANES] = sums[n].astype(BF16)

    def cot_edges():
        @pl.when(has_prev)
        def _():
            cot_up().wait_recv()

        @pl.when(has_next)
        def _():
            cot_down().wait_recv()

    def first_grads():
        total_ref[...] = grads(core, True)

    def last_grads():
        merge(total_ref[...] + grads(1 - core, False))

    def finish():
        for k in range(chips):
            core_copy(k).wait_send()
        if mid > 1:
            sent(zsend_ref.at[0 : mid - 1], z_s.at[0])
        sent(zsend_ref.at[0:mid], z_s.at[3])

        @pl.when(is_gate)
        def _():
            sent(zsend_ref.at[0:mid], z_s.at[2])
            for j in range(1, mid):
                sent(zsend_ref.at[0:mid], gr_s.at[j - 1])

        @pl.when(jnp.logical_not(is_gate))
        def _():
            sent(zsend_ref.at[0:mid], z_s.at[1])

        for side in range(2):

            @pl.when(edges(side))
            def _():
                sent(hrecv_ref.at[side, 0:mid], h_s.at[side])

            @pl.when(edges(side) & is_gate)
            def _():
                sent(hrecv_ref.at[side, 0:mid], h_s.at[2 + side])

        for j in range(1, chips):
            for p in range(2):
                x_copy(j, p).wait_send()
            sent(every_ref.at[:, 0:rows], gx_s.at[j - 1])
        sent(every_ref.at[:, 0 : chips * rows], gc_s.at[0])

        @pl.when(has_prev)
        def _():
            cot_down().wait_send()

        @pl.when(has_next)
        def _():
            cot_up().wait_send()

    green(0, 0)
    own_parts()
    core_sums()
    third_round()
    send_windows(2)
    green(1, 0)
    green(2, 0)
    loads[6].wait()
    cot_edges()
    backward(0)
    backward(1)
    all_here()
    gate_sums(2)
    core_copy(chip).wait_recv()
    sum_and_send(0)
    backward(2)
    relay(0)
    sum_and_send(1)
    spread_bins(z, 0)
    spread_bins(z, 1)
    relay(1)
    near_bins(0)
    near_bins(1)
    turn_shares()
    green(2, 1)
    gate_sums(0)
    green(0, 1)
    green(1, 1)
    gate_sums(1)
    relay(2)
    forward(2)
    far_bins(0)
    far_bins(1)
    forward(0)
    pass_bins(0)
    pass_bins(1)
    near_bins(2)
    far_bins(2)
    first_grads()
    forward(1)
    core_bins()
    last_grads()
    finish()


def store_kernel(signal_ref, grad_ref, signal_out, grad_out, sems):
    copies = (
        pltpu.make_async_copy(signal_ref, signal_out, sems.at[0]),
        pltpu.make_async_copy(grad_ref, grad_out, sems.at[1]),
    )
    for copy in copies:
        copy.start()
    for copy in copies:
        copy.wait()


def local(charge, intersection, ovl_block, ovl_count, diff_class, response, cotangent):
    blocks, planes, entries, wires, cells = intersection.shape
    bins = charge.shape[1]
    owners, slabs = lax.axis_size("gz"), lax.axis_size("drift")
    here, ticks_here = cotangent.shape[1:]
    spread, length = response.shape[1:]
    chips = owners // 2
    rows = 2 * here
    bins_here = bins // slabs
    block = math.gcd(ticks_here, 2 * LANES)
    pairs = (spread + 1) // 2
    front = (length - 1 + REACH + (TPB - 1) // 2) // TPB
    least = front
    while (LOW - TPB * front) % LANES >= TPB:
        front += 1
    taps_rows = round_up(2 * pairs, 8)
    depth = round_up(length, ROWS)
    assert owners % 2 == 0 and slabs % 2 == 0 and planes == 3
    assert front - least >= 2 and front + bins_here + HB <= LANES
    assert block * (ticks_here // block - 1) // TPB + WIN <= LANES
    assert length - 1 + REACH + (TPB - 1) // 2 - LOW < 2 * LANES
    dma = pltpu.SemaphoreType.DMA
    others = max(chips - 1, 1)
    mid = slabs // 2
    signal, charge_grad = pl.pallas_call(
        functools.partial(kernel, (owners, slabs, front, pairs, block)),
        out_shape=(
            jax.ShapeDtypeStruct((planes, here, ticks_here), BF16),
            jax.ShapeDtypeStruct((blocks * cells, bins), BF16),
        ),
        in_specs=[HBM] * 7,
        out_specs=(VMEM, VMEM),
        scratch_shapes=[
            pltpu.SMEM((planes, entries, blocks), jnp.int32),
            pltpu.SMEM(ovl_count.shape, jnp.int32),
            pltpu.VMEM(charge.shape, BF16),
            pltpu.VMEM(intersection.shape, BF16),
            pltpu.VMEM(diff_class.shape, jnp.int32),
            pltpu.VMEM(response.shape, BF16),
            pltpu.VMEM(cotangent.shape, BF16),
            dma((7,)),
            pltpu.SemaphoreType.REGULAR((2,)),
            pltpu.VMEM((owners * rows + here, blocks * cells), BF16),
            pltpu.VMEM((chips, rows, bins), F32),
            pltpu.VMEM((chips, rows, bins), BF16),
            pltpu.VMEM((chips, rows, bins), BF16),
            pltpu.VMEM((others, 2, here, bins), BF16),
            pltpu.VMEM((others, 2, here, bins), BF16),
            pltpu.VMEM((bins, slabs * LANES), BF16),
            pltpu.VMEM((slabs, planes, here, LANES), BF16),
            pltpu.VMEM((mid, planes, here, LANES), BF16),
            pltpu.VMEM((max(mid - 1, 1), mid, planes, here, LANES), BF16),
            pltpu.VMEM((mid, planes, here, LANES), BF16),
            pltpu.VMEM((2, mid + 1, planes, ROWS, LANES), BF16),
            pltpu.VMEM((2, planes, ROWS, ticks_here), BF16),
            pltpu.VMEM((slabs, owners * rows + here, LANES), BF16),
            pltpu.VMEM((blocks * cells, owners * rows + here), BF16),
            pltpu.VMEM((planes, taps_rows, depth), F32),
            pltpu.VMEM((2, planes * taps_rows * (NDIFF + 2), LANES), F32),
            pltpu.VMEM((2, planes, 2 * pairs, LANES, 4 * LANES), BF16),
            pltpu.VMEM((here + 2 * ROWS, 2 * pairs * WIN), F32),
            pltpu.VMEM((planes, here + 2 * ROWS + 8, LANES), F32),
            pltpu.VMEM((here + 2 * ROWS, LANES), F32),
            pltpu.VMEM((blocks * cells, slabs * LANES), F32),
            dma((chips,)),
            dma((chips,)),
            dma((others, 2)),
            dma((others, 2)),
            dma((4,)),
            dma((mid, planes)),
            dma((max(mid - 1, 1), planes)),
            dma((4,)),
            dma((2, planes)),
            dma((2,)),
            dma((2,)),
            dma((slabs, planes)),
            dma((max(mid - 1, 1),)),
            dma((others,)),
            dma((others, slabs, 2)),
            dma((2,)),
        ],
        compiler_params=pltpu.CompilerParams(
            collective_id=0, has_side_effects=True, vmem_limit_bytes=LIMIT * 1024 * 1024
        ),
        name="planes",
    )(
        *(
            pltpu.with_memory_space_constraint(array, pltpu.HBM)
            for array in (
                jnp.transpose(ovl_block, (1, 2, 0)),
                ovl_count,
                charge,
                intersection,
                diff_class,
                response,
                cotangent,
            )
        ),
    )
    return pl.pallas_call(
        store_kernel,
        out_shape=(
            jax.ShapeDtypeStruct(signal.shape, BF16),
            jax.ShapeDtypeStruct(charge_grad.shape, BF16),
        ),
        in_specs=[VMEM, VMEM],
        out_specs=(HBM, HBM),
        scratch_shapes=[pltpu.SemaphoreType.DMA((2,))],
        compiler_params=pltpu.CompilerParams(vmem_limit_bytes=4 * 1024 * 1024),
        name="store",
    )(signal, charge_grad)


def solution(mesh):
    return jax.shard_map(
        local,
        mesh=mesh,
        in_specs=(
            P(("apa", "gz", "drift"), None),
            P(("apa", "gz", "drift"), None, None, None, None),
            P(("apa", "gz", "drift"), None, None),
            P(("apa", "gz", "drift"), None),
            P("apa"),
            P(),
            P("apa", "gz", "drift"),
        ),
        out_specs=(P("apa", "gz", "drift"), P(("apa", "gz", "drift"), None)),
        check_vma=False,
    )
```
